32 devices in a mesh: areal: 8 (over y, x, core), layer: 4 (over z).
Axes of the slice: x: 2, y: 2, z: 4, core: 2. Of those that a mesh axis runs over, the one named last changes fastest.
Arguments:
- pressure: float32 [16, 128, 128], P('layer', 'areal'), may hold values from -4 to 4
- pressure_old: float32 [16, 128, 128], P('layer', 'areal'), may hold values from -4 to 4
- saturations: float32 [2, 16, 128, 128], P(None, 'layer', 'areal'), may hold values from 0.05 to 0.45
- saturations_old: float32 [2, 16, 128, 128], P(None, 'layer', 'areal'), may hold values from 0.05 to 0.45
- pore_volume: float32 [16, 128, 128], P('layer', 'areal'), may hold values from 4 to 16
- trans: float32 [3, 16, 128, 128], P(None, 'layer', 'areal'), may hold values from 0.05 to 0.5
- upwind: int32 [3, 16, 128, 128], P(None, 'layer', 'areal'), may hold values from 0 to 1
- active: int32 [16, 128, 128], P('layer', 'areal'), may hold values 0 or 1
- fault_cell: int32 [4, 8, 8, 64], P('layer', 'areal'), may hold values from 0 to 8191, as said below
- fault_live: int32 [4, 8, 8, 64], P('layer', 'areal'), may hold values from 0 to 1, as said below
- fault_up: int32 [4, 8, 8, 64], P('layer', 'areal'), may hold values from 0 to 1, as said below
- fault_trans: float32 [4, 8, 8, 64], P('layer', 'areal'), may hold values from 0.05 to 0.5, as said below
Outputs:
- residual: float32 [3, 16, 128, 128], P(None, 'layer', 'areal')
- update: float32 [3, 16, 128, 128], P(None, 'layer', 'areal')
The draws below stay inside these ranges and needn't reach their ends.
Inputs may be any that keep to these rules, and one draw needn't show every extreme that they name: `fault_cell`: slot (l, i, j, s) and slot (l, j, i, s) are the same fault face; entries are cell numbers of the block. fault_live[l, i, j, s] = fault_live[l, j, i, s]; zero where i = j; the live slots of a pair come first; in every layer index some pairs have all 64 slots live. fault_up[l, i, j, s] = 1 - fault_up[l, j, i, s] where i != j. fault_trans[l, i, j, s] = fault_trans[l, j, i, s].
All inputs are finite; a program needn't handle non-finite values. No bound on the sum of `active` on one device may be relied on, other than what follows from the above.
Results may differ from the reference program's by a relative error of at most 0.0003.
Values sent between devices are 32-bit elements; how exact they have to be, the bound alone decides.
No kernel may reach another device: no remote copies, remote signals or barrier semaphores. Data moves between devices by JAX's collectives and lax.ppermute only.
A program may use at most 64 MiB of HBM per device.

```python
import math
import jax
import jax.numpy as jnp
from jax import lax

LZ = 4
RY = 16
NX = 128
CAP = 64
SWEEPS = 4
KRYLOV = 2
NZ = 16
NY = 128
PEERS = 8
BLOCKS = 4
CELLS = 8192


def fault_tables(key):
    key_cells = jax.random.fold_in(key, 101)
    key_count = jax.random.fold_in(key, 202)
    key_keep = jax.random.fold_in(key, 303)
    key_shift = jax.random.fold_in(key, 404)
    key_flag = jax.random.fold_in(key, 505)
    key_trans = jax.random.fold_in(key, 606)
    shape = (BLOCKS, PEERS, PEERS, CAP)
    pair_shape = (BLOCKS, PEERS, PEERS)
    cells = jax.random.randint(key_cells, shape, 0, CELLS, dtype=jnp.int32)
    counts = jax.random.randint(key_count, pair_shape, CAP // 2, CAP + 1, dtype=jnp.int32)
    keeping = jax.random.randint(key_keep, pair_shape, 0, 3, dtype=jnp.int32) != 0
    offsets = jax.random.randint(key_shift, (BLOCKS, 1, 1), 1, PEERS, dtype=jnp.int32)
    owner = lax.broadcasted_iota(jnp.int32, pair_shape, 1)
    partner = lax.broadcasted_iota(jnp.int32, pair_shape, 2)
    full_pair = (partner == (owner + offsets) % PEERS) | (owner == (partner + offsets) % PEERS)
    drawn = jnp.where(full_pair, CAP, jnp.where(keeping, counts, 0))
    upper_half = owner < partner
    paired = jnp.where(upper_half, drawn, jnp.swapaxes(drawn, 1, 2))
    paired = jnp.where(owner == partner, 0, paired)
    slot_no = lax.broadcasted_iota(jnp.int32, shape, 3)
    live = (slot_no < paired[..., None]).astype(jnp.int32)
    upper_four = upper_half[..., None]
    coins = jax.random.randint(key_flag, shape, 0, 2, dtype=jnp.int32)
    flags = jnp.where(upper_four, coins, 1 - jnp.swapaxes(coins, 1, 2))
    spread = jax.random.uniform(key_trans, shape, jnp.float32, 0.0, 1.0)
    transmit = 0.05 * jnp.exp(jnp.log(10.0) * spread)
    transmit = jnp.where(upper_four, transmit, jnp.swapaxes(transmit, 1, 2))
    return (cells, live, flags, transmit)


def draw_fault_cell(key, part):
    return fault_tables(key)[0]


def draw_fault_live(key, part):
    return fault_tables(key)[1]


def draw_fault_up(key, part):
    return fault_tables(key)[2]


def draw_fault_trans(key, part):
    return fault_tables(key)[3].astype(jnp.float32)


def place_ends(values, key, low, top_value):
    longest = values.shape.index(max(values.shape))
    spots = []
    for shift in (0, 1):
        where = [jax.random.randint(jax.random.fold_in(key, axis), (), 0, length) for axis, length in enumerate(values.shape)]
        where[longest] = (where[longest] + shift) % values.shape[longest]
        spots.append(tuple(where))
    return values.at[spots[0]].set(low).at[spots[1]].set(top_value)


def block_levels(key, dims, cuts, smallest, largest):
    def one(axis_at, shards_of):
        steps = jax.random.uniform(jax.random.fold_in(jax.random.fold_in(key, 6), axis_at), (shards_of,), jnp.float32, smallest / len(cuts), largest / len(cuts))
        return jnp.repeat(jnp.exp(steps), dims[axis_at] // shards_of).reshape((-1,) + (1,) * (len(dims) - axis_at - 1))

    gain = one(*cuts[0])
    for cut in cuts[1:]:
        gain = gain * one(*cut)
    return gain


def bell_draw(own_key, shape, deviation, most, cuts=(), kind=jnp.bfloat16):
    values = jax.random.normal(own_key, shape, jnp.float32) * deviation
    if len(cuts) > 0:
        values = block_levels(own_key, shape, cuts, -0.22, 0.18) * values
    return jnp.clip(values, min=-most, max=most).astype(kind)


def setup_inputs(seed: int = 0) -> dict:
    keys = jax.random.split(jax.random.key(seed), 13)
    pressure = bell_draw(keys[0], (NZ, NY, NX), 1.0, 4.0, ((0, 4), (1, 8)), jnp.float32)
    pressure_old = bell_draw(keys[1], (NZ, NY, NX), 1.0, 4.0, ((0, 4), (1, 8)), jnp.float32)
    saturations = jnp.clip(0.05 + 0.39999999 * jax.random.uniform(keys[2], (2, NZ, NY, NX), jnp.float32) ** block_levels(keys[2], (2, NZ, NY, NX), ((1, 4), (2, 8)), -0.2, 0.2), 0.05, 0.45)
    saturations_old = jnp.clip(0.05 + 0.39999999 * jax.random.uniform(keys[3], (2, NZ, NY, NX), jnp.float32) ** block_levels(keys[3], (2, NZ, NY, NX), ((1, 4), (2, 8)), -0.2, 0.2), 0.05, 0.45)
    pore_volume = jnp.clip(jnp.exp(math.log(16.0) - 1.3862944 * jax.random.uniform(keys[4], (NZ, NY, NX), jnp.float32) ** block_levels(keys[4], (NZ, NY, NX), ((0, 4), (1, 8)), -0.2, 0.2)), 4.0, 16.0)
    trans = jnp.clip(jnp.exp(math.log(0.5) - 2.3025851 * jax.random.uniform(keys[5], (3, NZ, NY, NX), jnp.float32) ** block_levels(keys[5], (3, NZ, NY, NX), ((1, 4), (2, 8)), -0.2, 0.2)), 0.05, 0.5)
    upwind = place_ends(jax.random.randint(keys[6], (3, NZ, NY, NX), 0, 2), jax.random.fold_in(keys[6], 1), 0, 1).astype(jnp.int32)
    active = place_ends((jax.random.randint(keys[7], (NZ, NY, NX), 0, 8) < 7).astype(jnp.int32), jax.random.fold_in(keys[7], 1), 0, 1)
    fault_cell = draw_fault_cell(jax.random.fold_in(keys[12], 71), 0)
    fault_live = draw_fault_live(jax.random.fold_in(keys[12], 71), 0)
    fault_up = draw_fault_up(jax.random.fold_in(keys[12], 71), 0)
    fault_trans = draw_fault_trans(jax.random.fold_in(keys[12], 71), 0)
    return dict(pressure=pressure, pressure_old=pressure_old, saturations=saturations, saturations_old=saturations_old, pore_volume=pore_volume, trans=trans, upwind=upwind, active=active, fault_cell=fault_cell, fault_live=fault_live, fault_up=fault_up, fault_trans=fault_trans)


VISCOSITY = (0.5, 2.0, 0.2)
COMPRESS = (0.01, 0.02, 0.05)
DAMPING = 0.7

def mobility(sat_water, sat_gas):
    sat_oil = 1.0 - sat_water - sat_gas
    mobile = jnp.stack([sat_water * sat_water / VISCOSITY[0], sat_oil * sat_oil / VISCOSITY[1], sat_gas * sat_gas / VISCOSITY[2]])
    slopes = jnp.stack([2.0 * sat_water / VISCOSITY[0], -2.0 * sat_oil / VISCOSITY[1], 2.0 * sat_gas / VISCOSITY[2]])
    return (mobile, slopes)

def row_change(move_water, move_gas):
    return jnp.stack([move_water, move_water + move_gas, move_gas])

def store_change(move_water, move_gas):
    return jnp.stack([move_water, -(move_water + move_gas), move_gas])

def split_faces(field, axis_no):
    middle = [slice(1, -1), slice(1, -1), slice(1, -1)]
    low_cut = list(middle)
    high_cut = list(middle)
    low_cut[axis_no] = slice(0, -1)
    high_cut[axis_no] = slice(1, None)
    leading = [slice(None)] * (field.ndim - 3)
    return (field[tuple(leading + low_cut)], field[tuple(leading + high_cut)])

def to_cells(term, axis_no):
    return jnp.diff(term, axis=term.ndim - 3 + axis_no)

def both_sides(term, axis_no):
    position = term.ndim - 3 + axis_no
    extent = term.shape[position]
    return lax.slice_in_dim(term, 1, extent, axis=position) + lax.slice_in_dim(term, 0, extent - 1, axis=position)

def face_terms(p_low, p_high, mob_low, mob_high, slope_low, slope_high, face_tau, upwind_high):
    drop = p_high - p_low
    mob_up = jnp.where(upwind_high, mob_high, mob_low)
    slope_up = jnp.where(upwind_high, slope_high, slope_low)
    flow = face_tau * mob_up
    bend = face_tau * drop * slope_up
    return (flow, bend, -flow * drop)

def grid_pad(field):
    return jnp.pad(field, ((0, 0),) * (field.ndim - 3) + ((1, 1), (1, 1), (1, 1)))

def pick_flat(field, index):
    return field.reshape(field.shape[:-3] + (-1,))[..., index]

def scatter_flat(term, index, cell_shape):
    leading = term.shape[:-1]
    cell_count = cell_shape[0] * cell_shape[1] * cell_shape[2]
    flat = jnp.zeros(leading + (cell_count,), jnp.float32).at[..., index].add(term)
    return flat.reshape(leading + tuple(cell_shape))

def global_index(block_no, owner_no, cell):
    layer_no = block_no * LZ + cell // (RY * NX)
    row_no = owner_no * RY + cell // NX % RY
    return ((layer_no * NY + row_no) * NX + cell % NX).astype(jnp.int32)

def least_squares(columns, beta):
    column_count = len(columns)
    target = [beta] + [0.0] * column_count
    rotations = []
    reduced = []
    for col_no in range(column_count):
        column = list(columns[col_no])
        for rot_no in range(len(rotations)):
            cosine, sine_part = rotations[rot_no]
            entry_top = column[rot_no]
            entry_low = column[rot_no + 1]
            column[rot_no] = cosine * entry_top + sine_part * entry_low
            column[rot_no + 1] = -sine_part * entry_top + cosine * entry_low
        radius = jnp.sqrt(column[col_no] * column[col_no] + column[col_no + 1] * column[col_no + 1])
        cosine = column[col_no] / radius
        sine_part = column[col_no + 1] / radius
        column[col_no] = radius
        rotations.append((cosine, sine_part))
        entry_top = target[col_no]
        entry_low = target[col_no + 1]
        target[col_no] = cosine * entry_top + sine_part * entry_low
        target[col_no + 1] = -sine_part * entry_top + cosine * entry_low
        reduced.append(column)
    weights = [None] * column_count
    for row_no in reversed(range(column_count)):
        running = target[row_no]
        for col_no in range(row_no + 1, column_count):
            running = running - reduced[col_no][row_no] * weights[col_no]
        weights[row_no] = running / reduced[row_no][row_no]
    return weights

def reference(pressure, pressure_old, saturations, saturations_old, pore_volume, trans, upwind, active, fault_cell, fault_live, fault_up, fault_trans):
    cell_shape = pressure.shape
    blocks = lax.broadcasted_iota(jnp.int32, fault_cell.shape, 0)
    owners = lax.broadcasted_iota(jnp.int32, fault_cell.shape, 1)
    partners = lax.broadcasted_iota(jnp.int32, fault_cell.shape, 2)
    mine_index = global_index(blocks, owners, fault_cell).reshape(-1)
    their_index = global_index(blocks, partners, jnp.swapaxes(fault_cell, 1, 2)).reshape(-1)
    fault_high = fault_up.reshape(-1) > 0
    act = active.astype(jnp.float32)
    spare = 1.0 - act
    sat_water = saturations[0]
    sat_gas = saturations[1]
    compress = jnp.array(COMPRESS, jnp.float32).reshape(3, 1, 1, 1)
    change = pressure - pressure_old
    sat_now = jnp.stack([sat_water, 1.0 - sat_water - sat_gas, sat_gas])
    sat_before = jnp.stack([saturations_old[0], 1.0 - saturations_old[0] - saturations_old[1], saturations_old[1]])
    store_p = act * pore_volume * compress * sat_now
    store_s = pore_volume * (1.0 + compress * change)
    accum = pore_volume * (sat_now - sat_before + compress * sat_now * change)
    state_four = jnp.stack([pressure, sat_water, sat_gas, act])
    rimmed = grid_pad(state_four)
    trans_pad = grid_pad(trans)
    flag_pad = grid_pad(upwind.astype(jnp.float32))
    mob_all, slope_all = mobility(rimmed[1], rimmed[2])
    resid = act * accum
    diag_p = lax.optimization_barrier(jnp.sum(store_p, axis=0))
    face_list = []
    for axis_no, trans_no in ((2, 0), (1, 1), (0, 2)):
        p_low, p_high = split_faces(rimmed[0], axis_no)
        act_low, act_high = split_faces(rimmed[3], axis_no)
        mob_low, mob_high = split_faces(mob_all, axis_no)
        slope_low, slope_high = split_faces(slope_all, axis_no)
        trans_low = split_faces(trans_pad[trans_no], axis_no)[0]
        high_side = split_faces(flag_pad[trans_no], axis_no)[0] > 0.5
        flow, bend, face_resid = face_terms(p_low, p_high, mob_low, mob_high, slope_low, slope_high, trans_low * act_low * act_high, high_side)
        resid = resid + to_cells(face_resid, axis_no)
        flow_total = lax.optimization_barrier(jnp.sum(flow, axis=0))
        diag_p = diag_p + both_sides(flow_total, axis_no)
        face_list.append((axis_no, flow, flow_total, bend, high_side))
    mine = pick_flat(state_four, mine_index)
    theirs = pick_flat(state_four, their_index)
    mob_mine, slope_mine = mobility(mine[1], mine[2])
    mob_their, slope_their = mobility(theirs[1], theirs[2])
    fault_tau = fault_trans.reshape(-1) * fault_live.reshape(-1).astype(jnp.float32) * mine[3] * theirs[3]
    fault_flow, fault_bend, fault_resid = face_terms(mine[0], theirs[0], mob_mine, mob_their, slope_mine, slope_their, fault_tau, fault_high)
    resid = resid + scatter_flat(fault_resid, mine_index, cell_shape)
    diag_p = diag_p + scatter_flat(lax.optimization_barrier(jnp.sum(fault_flow, axis=0)), mine_index, cell_shape) + spare

    def pressure_rows(field):
        rimmed_q = grid_pad(field)
        zeros_field = jnp.zeros_like(field)
        rows = store_p * field + jnp.stack([spare * field, zeros_field, zeros_field])
        for axis_no, flow, flow_total, bend, high_side in face_list:
            low_part, high_part = split_faces(rimmed_q, axis_no)
            rows = rows + to_cells(flow * (low_part - high_part), axis_no)
        gap = pick_flat(field, mine_index) - pick_flat(field, their_index)
        return rows + scatter_flat(fault_flow * gap, mine_index, cell_shape)

    def pressure_op(field):
        rimmed_q = grid_pad(field)
        total = lax.optimization_barrier(jnp.sum(store_p, axis=0)) * field + spare * field
        for axis_no, flow, flow_total, bend, high_side in face_list:
            low_part, high_part = split_faces(rimmed_q, axis_no)
            total = total + to_cells(flow_total * (low_part - high_part), axis_no)
        gap = pick_flat(field, mine_index) - pick_flat(field, their_index)
        return total + scatter_flat(lax.optimization_barrier(jnp.sum(fault_flow, axis=0)) * gap, mine_index, cell_shape)

    def sat_rows(moves):
        rimmed_s = grid_pad(moves)
        zeros_field = jnp.zeros_like(moves[0])
        rows = act * store_s * store_change(moves[0], moves[1]) + jnp.stack([zeros_field, spare * moves[0], spare * moves[1]])
        for axis_no, flow, flow_total, bend, high_side in face_list:
            low_part, high_part = split_faces(rimmed_s, axis_no)
            upwind_part = jnp.where(high_side, high_part, low_part)
            rows = rows - to_cells(bend * row_change(upwind_part[0], upwind_part[1]), axis_no)
        upwind_fault = jnp.where(fault_high, pick_flat(moves, their_index), pick_flat(moves, mine_index))
        return rows - scatter_flat(fault_bend * row_change(upwind_fault[0], upwind_fault[1]), mine_index, cell_shape)

    def precondition(vector):
        rhs_p = lax.optimization_barrier(jnp.sum(vector, axis=0))
        guess = DAMPING * rhs_p / diag_p
        for sweep_no in range(SWEEPS - 1):
            guess = guess + DAMPING * (rhs_p - pressure_op(guess)) / diag_p
        second = vector - pressure_rows(guess)
        return jnp.stack([guess, act * second[0] / store_s[0], act * second[2] / store_s[2]])
    start = -resid
    beta = jnp.sqrt(jnp.sum(start * start))
    basis = [start / beta]
    directions = []
    columns = []
    for col_no in range(KRYLOV):
        prec = precondition(basis[-1])
        image = pressure_rows(prec[0]) + sat_rows(prec[1:])
        projections = [jnp.sum(image * vec) for vec in basis]
        remain = image
        for row_no in range(len(projections)):
            remain = remain - projections[row_no] * basis[row_no]
        height = jnp.sqrt(jnp.sum(remain * remain))
        columns.append(projections + [height])
        directions.append(prec)
        basis.append(remain / height)
    weights = least_squares(columns, beta)
    update = weights[0] * directions[0]
    for col_no in range(1, KRYLOV):
        update = update + weights[col_no] * directions[col_no]
    return (resid, update)
```

```python
import functools

import jax
import jax.numpy as jnp
from jax import lax
from jax.experimental import pallas as pl
from jax.experimental.pallas import tpu as pltpu
from jax.sharding import PartitionSpec as P

SWEEPS = 4

COMPRESS = (0.01, 0.02, 0.05)
DAMPING = 0.7

F32 = jnp.float32
BF16 = jnp.bfloat16


class Sizes:
    def __init__(self, areal, layer, cells, cap):
        self.areal = areal
        self.layer = layer
        self.lz, self.ry, self.nx = cells
        self.cap = cap
        self.rows = self.lz * self.ry
        self.slots = areal * cap

    def block_rows(self, y_fields, slot_fields):
        used = y_fields * self.lz + slot_fields
        return -(-used // 8) * 8


def iota(shape, dim):
    return lax.broadcasted_iota(jnp.int32, shape, dim)


def layers_of(sz, ref, *lead):
    return [ref[lead + (no,)] for no in range(sz.lz)]


def put_layers(ref, lead, parts):
    for no, part in enumerate(parts):
        ref[lead + (no,)] = part


def split_parts(value):
    high = value.astype(BF16)
    rest = value - high.astype(F32)
    middle = rest.astype(BF16)
    low = (rest - middle.astype(F32)).astype(BF16)
    return high, middle, low


def gather_slots(sz, fields, row_hot, col_hot):
    pieces = [split_parts(jnp.concatenate(field, axis=0)) for field in fields]
    lhs = jnp.concatenate([part for piece in pieces for part in piece], axis=0)
    picked = jnp.dot(lhs, col_hot, preferred_element_type=F32)
    out = []
    for no in range(len(fields)):
        base = 3 * no * sz.rows
        high = picked[base : base + sz.rows]
        middle = picked[base + sz.rows : base + 2 * sz.rows]
        low = picked[base + 2 * sz.rows : base + 3 * sz.rows]
        full = (low + middle) + high
        out.append(jnp.sum(full * row_hot, axis=0, keepdims=True))
    return jnp.concatenate(out, axis=0)


def scatter_slots(sz, values, row_hot, col_hot):
    count = values.shape[0]
    pieces = []
    for no in range(count):
        value = values[no : no + 1]
        high = value.astype(BF16).astype(F32)
        rest = value - high
        middle = rest.astype(BF16).astype(F32)
        low = (rest - middle).astype(BF16).astype(F32)
        for part in (high, middle, low):
            pieces.append((row_hot * part).astype(BF16))
    lhs = jnp.concatenate(pieces, axis=0)
    spread = lax.dot_general(
        lhs, col_hot, (((1,), (1,)), ((), ())), preferred_element_type=F32
    )
    out = []
    for no in range(count):
        base = 3 * no * sz.rows
        high = spread[base : base + sz.rows]
        middle = spread[base + sz.rows : base + 2 * sz.rows]
        low = spread[base + 2 * sz.rows : base + 3 * sz.rows]
        full = (low + middle) + high
        out.append([full[k * sz.ry : (k + 1) * sz.ry] for k in range(sz.lz)])
    return out


def lane_row(sz, ref):
    return jnp.concatenate([ref[0, 0, j : j + 1, :] for j in range(sz.areal)], axis=1)


def read_slots(sz, recv_ref, first, count):
    return jnp.concatenate(
        [recv_ref[j, first : first + count, 0 : sz.cap] for j in range(sz.areal)], axis=1
    )


def write_slots(sz, send_ref, first, values):
    count = values.shape[0]
    for j in range(sz.areal):
        send_ref[j, first : first + count, 0 : sz.cap] = values[:, j * sz.cap : (j + 1) * sz.cap]


def even_layer(sz):
    place = lax.rem(lax.axis_index("layer"), 2)
    return jnp.full((sz.ry, sz.nx), place, jnp.int32) == 0


def write_halo(sz, send_ref, even_ref, odd_ref, y_up, y_down, z_up, z_down):
    me = lax.axis_index("areal")

    @pl.when(me < sz.areal - 1)
    def _():
        for f, field in enumerate(y_up):
            for k in range(sz.lz):
                send_ref[me + 1, f * sz.lz + k : f * sz.lz + k + 1, :] = field[k][sz.ry - 1 : sz.ry]

    @pl.when(me > 0)
    def _():
        for f, field in enumerate(y_down):
            for k in range(sz.lz):
                send_ref[me - 1, f * sz.lz + k : f * sz.lz + k + 1, :] = field[k][0:1]

    even = even_layer(sz)
    for f in range(len(z_up)):
        top = z_up[f][sz.lz - 1]
        bottom = z_down[f][0] if f < len(z_down) else top
        even_ref[f] = jnp.where(even, top, bottom)
        odd_ref[f] = jnp.where(even, bottom, top)


def read_halo(sz, recv_ref, even_ref, odd_ref, low_fields, high_fields):
    me = lax.axis_index("areal")
    has_low = jnp.full((1, sz.nx), me, jnp.int32) > 0
    has_high = jnp.full((1, sz.nx), me, jnp.int32) < sz.areal - 1
    before = jnp.maximum(me - 1, 0)
    after = jnp.minimum(me + 1, sz.areal - 1)
    even = even_layer(sz)
    lows, highs = [], []
    for f in range(low_fields):
        y_part = [
            jnp.where(has_low, recv_ref[before, f * sz.lz + k : f * sz.lz + k + 1, :], 0.0)
            for k in range(sz.lz)
        ]
        lows.append((y_part, jnp.where(even, odd_ref[f], even_ref[f])))
    for f in range(high_fields):
        y_part = [
            jnp.where(has_high, recv_ref[after, f * sz.lz + k : f * sz.lz + k + 1, :], 0.0)
            for k in range(sz.lz)
        ]
        highs.append((y_part, jnp.where(even, even_ref[f], odd_ref[f])))
    return lows, highs


def x_below(sz, part):
    return pltpu.roll(part, 1, 1)


def x_above(sz, part):
    return pltpu.roll(part, sz.nx - 1, 1)


def y_below(sz, part, edge):
    return jnp.where(iota((sz.ry, sz.nx), 0) == 0, edge, pltpu.roll(part, 1, 0))


def y_above(sz, part, edge):
    return jnp.where(iota((sz.ry, sz.nx), 0) == sz.ry - 1, edge, pltpu.roll(part, sz.ry - 1, 0))


def neighbours(sz, field, k, low, high):
    below = field[k - 1] if k > 0 else low[1]
    above = field[k + 1] if k < sz.lz - 1 else high[1]
    return (
        x_below(sz, field[k]),
        x_above(sz, field[k]),
        y_below(sz, field[k], low[0][k]),
        y_above(sz, field[k], high[0][k]),
        below,
        above,
    )


def mobility(sat_water, sat_gas):
    sat_oil = 1.0 - sat_water - sat_gas
    mobile = (
        sat_water * sat_water * 2.0,
        sat_oil * sat_oil * 0.5,
        sat_gas * sat_gas * 5.0,
    )
    slopes = (4.0 * sat_water, -sat_oil, 10.0 * sat_gas)
    return mobile, slopes


def pack_kernel(
    sz, p_ref, sat_ref, act_ref, trans_ref, up_ref, cell_ref,
    send_ref, even_ref, odd_ref, col_ref, row_ref, mine_ref,
):
    cell = lane_row(sz, cell_ref)
    row_start = iota((sz.rows, sz.slots), 0) * sz.nx
    in_row = (cell >= row_start) & (cell < row_start + sz.nx)
    row_hot = jnp.where(in_row, 1.0, 0.0)
    column = cell - jnp.sum(jnp.where(in_row, row_start, 0), axis=0, keepdims=True)
    col_hot = jnp.where(iota((sz.nx, sz.slots), 0) == column, 1.0, 0.0).astype(BF16)
    row_ref[...] = row_hot
    col_ref[...] = col_hot
    pressure = layers_of(sz, p_ref)
    water = layers_of(sz, sat_ref, 0)
    gas = layers_of(sz, sat_ref, 1)
    act = [part.astype(F32) for part in layers_of(sz, act_ref)]
    ty = [t * a for t, a in zip(layers_of(sz, trans_ref, 1), act)]
    tz = [t * a for t, a in zip(layers_of(sz, trans_ref, 2), act)]
    uy = [u.astype(F32) for u in layers_of(sz, up_ref, 1)]
    uz = [u.astype(F32) for u in layers_of(sz, up_ref, 2)]
    four = [pressure, water, gas, act]
    write_halo(
        sz, send_ref, even_ref, odd_ref,
        [pressure, water, gas, ty, uy], four, [pressure, water, gas, tz, uz], four,
    )
    mine = gather_slots(sz, four, row_hot, col_hot)
    mine_ref[...] = mine
    write_slots(sz, send_ref, 5 * sz.lz, mine)


def setup_kernel(
    sz, recv_ref, even_in, odd_in, p_ref, old_ref, sat_ref, sat_old_ref, pore_ref, trans_ref,
    up_ref, act_ref, live_ref, fup_ref, ftrans_ref, col_ref, row_ref, mine_ref,
    resid_ref, start_ref, total_ref, image_ref, sat_co_ref, inv_ref, slot_ref,
    rhs_ref, guess_ref, send_ref, even_ref, odd_ref,
):
    row_hot = row_ref[...]
    col_hot = col_ref[...]
    mine = mine_ref[...]
    their = read_slots(sz, recv_ref, 5 * sz.lz, 4)
    live = lane_row(sz, live_ref).astype(F32)
    high = lane_row(sz, fup_ref) > 0
    tau = lane_row(sz, ftrans_ref) * live * mine[3:4] * their[3:4]
    drop = their[0:1] - mine[0:1]
    mobile, slopes = mobility(
        jnp.where(high, their[1:2], mine[1:2]), jnp.where(high, their[2:3], mine[2:3])
    )
    flow = [tau * part for part in mobile]
    bend = [tau * drop * part for part in slopes]
    flow_sum = flow[0] + flow[1] + flow[2]
    slot_ref[...] = jnp.concatenate(
        [flow_sum]
        + flow
        + [jnp.where(high, 0.0, part) for part in bend]
        + [jnp.where(high, part, 0.0) for part in bend],
        axis=0,
    )
    scattered = scatter_slots(
        sz,
        jnp.concatenate(flow + [part * drop for part in flow], axis=0),
        row_hot,
        col_hot,
    )
    lows, highs = read_halo(sz, recv_ref, even_in, odd_in, 5, 4)
    pressure = layers_of(sz, p_ref)
    water = layers_of(sz, sat_ref, 0)
    gas = layers_of(sz, sat_ref, 1)
    act = [part.astype(F32) for part in layers_of(sz, act_ref)]
    trans = [layers_of(sz, trans_ref, axis) for axis in range(3)]
    flags = [[u.astype(F32) for u in layers_of(sz, up_ref, axis)] for axis in range(3)]
    carried = [[t * a for t, a in zip(trans[axis], act)] for axis in range(3)]
    lane = iota((sz.ry, sz.nx), 1)
    guesses = []
    for k in range(sz.lz):
        own_act = act[k]
        spare = 1.0 - own_act
        near = [
            neighbours(sz, field, k, lows[f], highs[f])
            for f, field in enumerate((pressure, water, gas, act))
        ]
        below_y = y_below(sz, carried[1][k], lows[3][0][k])
        flag_y = y_below(sz, flags[1][k], lows[4][0][k])
        below_z = carried[2][k - 1] if k > 0 else lows[3][1]
        flag_z = flags[2][k - 1] if k > 0 else lows[4][1]
        taus = (
            jnp.where(lane > 0, x_below(sz, carried[0][k]) * own_act, 0.0),
            jnp.where(lane < sz.nx - 1, carried[0][k] * near[3][1], 0.0),
            below_y * own_act,
            carried[1][k] * near[3][3],
            below_z * own_act,
            carried[2][k] * near[3][5],
        )
        other_up = (
            x_below(sz, flags[0][k]) < 0.5,
            flags[0][k] > 0.5,
            flag_y < 0.5,
            flags[1][k] > 0.5,
            flag_z < 0.5,
            flags[2][k] > 0.5,
        )
        change = pressure[k] - old_ref[k]
        oil = 1.0 - water[k] - gas[k]
        old_water = sat_old_ref[0, k]
        old_gas = sat_old_ref[1, k]
        now = (water[k], oil, gas[k])
        before = (old_water, 1.0 - old_water - old_gas, old_gas)
        pore = pore_ref[k]
        store_p = [own_act * pore * c * s for c, s in zip(COMPRESS, now)]
        store_s = [pore * (1.0 + c * change) for c in COMPRESS]
        resid = [
            own_act * (pore * (s - b + c * s * change)) for c, s, b in zip(COMPRESS, now, before)
        ]
        image_own = [store_p[0], store_p[1], store_p[2]]
        sat_own = [own_act * store_s[0], -(own_act * store_s[1]), own_act * store_s[2]]
        diag = store_p[0] + store_p[1] + store_p[2]
        for d in range(6):
            step = near[0][d] - pressure[k]
            mobile, slopes = mobility(
                jnp.where(other_up[d], near[1][d], water[k]),
                jnp.where(other_up[d], near[2][d], gas[k]),
            )
            face_flow = [taus[d] * part for part in mobile]
            total = face_flow[0] + face_flow[1] + face_flow[2]
            total_ref[d, k] = total
            diag = diag + total
            slope_tau = taus[d] * step
            for row in range(3):
                resid[row] = resid[row] - face_flow[row] * step
                image_own[row] = image_own[row] + face_flow[row]
                image_ref[3 + 6 * row + d, k] = face_flow[row]
                face_bend = slope_tau * slopes[row]
                sat_co_ref[4 + 6 * row + d, k] = jnp.where(other_up[d], face_bend, 0.0)
                sat_own[row] = sat_own[row] - jnp.where(other_up[d], 0.0, face_bend)
        for row in range(3):
            resid[row] = resid[row] - scattered[3 + row][k]
            image_own[row] = image_own[row] + scattered[row][k]
            resid_ref[row, k] = resid[row]
            start_ref[row, k] = -resid[row]
        diag = diag + (scattered[0][k] + scattered[1][k] + scattered[2][k]) + spare
        image_ref[0, k] = image_own[0] + spare
        image_ref[1, k] = image_own[1]
        image_ref[2, k] = image_own[2]
        sat_co_ref[0, k] = sat_own[0]
        sat_co_ref[1, k] = sat_own[1]
        sat_co_ref[2, k] = sat_own[2] + spare
        sat_co_ref[3, k] = spare
        relax = DAMPING / diag
        inv_ref[0, k] = relax
        inv_ref[1, k] = own_act / store_s[0]
        inv_ref[2, k] = own_act / store_s[2]
        rhs = -(resid[0] + resid[1] + resid[2])
        rhs_ref[k] = rhs
        guess = relax * rhs
        guess_ref[k] = guess
        guesses.append(guess)
    send_one(sz, guesses, row_hot, col_hot, send_ref, even_ref, odd_ref)


def send_one(sz, field, row_hot, col_hot, send_ref, even_ref, odd_ref):
    write_halo(sz, send_ref, even_ref, odd_ref, [field], [field], [field], [field])
    write_slots(sz, send_ref, sz.lz, gather_slots(sz, [field], row_hot, col_hot))


def sweep_kernel(
    sz, recv_ref, even_in, odd_in, guess_in, rhs_ref, total_ref, inv_ref, slot_ref, col_ref,
    row_ref, guess_ref, send_ref, even_ref, odd_ref,
):
    row_hot = row_ref[...]
    col_hot = col_ref[...]
    their = read_slots(sz, recv_ref, sz.lz, 1)
    scattered = scatter_slots(sz, slot_ref[0:1] * their, row_hot, col_hot)[0]
    lows, highs = read_halo(sz, recv_ref, even_in, odd_in, 1, 1)
    old = layers_of(sz, guess_in)
    guesses = []
    for k in range(sz.lz):
        near = neighbours(sz, old, k, lows[0], highs[0])
        total = rhs_ref[k]
        for d in range(6):
            total = total + total_ref[d, k] * near[d]
        total = total + scattered[k]
        guess = (1.0 - DAMPING) * old[k] + inv_ref[0, k] * total
        guess_ref[k] = guess
        guesses.append(guess)
    send_one(sz, guesses, row_hot, col_hot, send_ref, even_ref, odd_ref)


def second_kernel(
    sz, recv_ref, even_in, odd_in, guess_in, vector_ref, image_co_ref, inv_ref, slot_ref, col_ref,
    row_ref, image_ref, moves_ref, picked_ref, send_ref, even_ref, odd_ref,
):
    row_hot = row_ref[...]
    col_hot = col_ref[...]
    their = read_slots(sz, recv_ref, sz.lz, 1)
    scattered = scatter_slots(sz, slot_ref[1:4] * their, row_hot, col_hot)
    lows, highs = read_halo(sz, recv_ref, even_in, odd_in, 1, 1)
    guess = layers_of(sz, guess_in)
    water, gas = [], []
    for k in range(sz.lz):
        near = neighbours(sz, guess, k, lows[0], highs[0])
        for row in range(3):
            value = image_co_ref[row, k] * guess[k]
            for d in range(6):
                value = value - image_co_ref[3 + 6 * row + d, k] * near[d]
            value = value - scattered[row][k]
            image_ref[row, k] = value
            if row == 0:
                move = inv_ref[1, k] * (vector_ref[0, k] - value)
                moves_ref[0, k] = move
                water.append(move)
            if row == 2:
                move = inv_ref[2, k] * (vector_ref[2, k] - value)
                moves_ref[1, k] = move
                gas.append(move)
    both = [water, gas]
    write_halo(sz, send_ref, even_ref, odd_ref, both, both, both, both)
    picked = gather_slots(sz, both, row_hot, col_hot)
    picked_ref[...] = picked
    write_slots(sz, send_ref, 2 * sz.lz, picked)


def apply_sat(sz, recv_ref, even_in, odd_in, moves_ref, picked_ref, image_ref, co_ref, slot_ref,
              col_hot, row_hot):
    their = read_slots(sz, recv_ref, 2 * sz.lz, 2)
    mine = picked_ref[...]
    mine_rows = (mine[0:1], mine[0:1] + mine[1:2], mine[1:2])
    their_rows = (their[0:1], their[0:1] + their[1:2], their[1:2])
    values = jnp.concatenate(
        [
            slot_ref[4 + row : 5 + row] * mine_rows[row]
            + slot_ref[7 + row : 8 + row] * their_rows[row]
            for row in range(3)
        ],
        axis=0,
    )
    scattered = scatter_slots(sz, values, row_hot, col_hot)
    lows, highs = read_halo(sz, recv_ref, even_in, odd_in, 2, 2)
    water = layers_of(sz, moves_ref, 0)
    gas = layers_of(sz, moves_ref, 1)
    rows = []
    for k in range(sz.lz):
        near_w = neighbours(sz, water, k, lows[0], highs[0])
        near_g = neighbours(sz, gas, k, lows[1], highs[1])
        near = (near_w, [w + g for w, g in zip(near_w, near_g)], near_g)
        own = (water[k], water[k] + gas[k], gas[k])
        layer_rows = []
        for row in range(3):
            value = image_ref[row, k] + co_ref[row, k] * own[row]
            if row == 1:
                value = value + co_ref[3, k] * water[k]
            for d in range(6):
                value = value - co_ref[4 + 6 * row + d, k] * near[row][d]
            layer_rows.append(value - scattered[row][k])
        rows.append(layer_rows)
    return rows


def next_kernel(
    sz, recv_ref, even_in, odd_in, moves_ref, picked_ref, image_ref, vector_ref, co_ref, inv_ref,
    slot_ref, col_ref, row_ref, shifted_ref, rhs_ref, guess_ref, send_ref, even_ref, odd_ref,
):
    row_hot = row_ref[...]
    col_hot = col_ref[...]
    rows = apply_sat(
        sz, recv_ref, even_in, odd_in, moves_ref, picked_ref, image_ref, co_ref, slot_ref, col_hot,
        row_hot,
    )
    guesses = []
    for k in range(sz.lz):
        shifted = [rows[k][row] - vector_ref[row, k] for row in range(3)]
        for row in range(3):
            shifted_ref[row, k] = shifted[row]
        rhs = shifted[0] + shifted[1] + shifted[2]
        rhs_ref[k] = rhs
        guess = inv_ref[0, k] * rhs
        guess_ref[k] = guess
        guesses.append(guess)
    send_one(sz, guesses, row_hot, col_hot, send_ref, even_ref, odd_ref)


def gram_kernel(
    sz, recv_ref, even_in, odd_in, moves_ref, picked_ref, image_ref, start_ref, vector_ref, co_ref,
    slot_ref, col_ref, row_ref, sums_ref,
):
    rows = apply_sat(
        sz, recv_ref, even_in, odd_in, moves_ref, picked_ref, image_ref, co_ref, slot_ref,
        col_ref[...], row_ref[...],
    )
    sums = [jnp.zeros((sz.ry, sz.nx), F32) for _ in range(6)]
    for k in range(sz.lz):
        for row in range(3):
            first = start_ref[row, k]
            second = vector_ref[row, k]
            third = rows[k][row] - second
            pairs = (
                (first, first), (first, second), (second, second),
                (first, third), (second, third), (third, third),
            )
            sums = [total + a * b for total, (a, b) in zip(sums, pairs)]
    lane = iota((1, sz.nx), 1)
    line = jnp.zeros((1, sz.nx), F32)
    for no, total in enumerate(sums):
        value = jnp.sum(jnp.sum(total, axis=0, keepdims=True), axis=1, keepdims=True)
        line = jnp.where(lane == no, value, line)
    sums_ref[...] = jnp.broadcast_to(line.reshape(1, 1, sz.nx), sums_ref.shape)


def weights_of(gram):
    rr, rx, xx, ry, xy, yy = gram
    beta = jnp.sqrt(rr)
    along = rx / rr
    norm_sq = jnp.maximum(xx - along * rx, 0.0)
    norm = jnp.sqrt(norm_sq)
    h11 = 1.0 + along
    h21 = norm / beta
    on_first = (ry - along * rx) / (norm * beta)
    on_second = (xy - along * xx - along * ry + along * along * rx) / norm_sq
    length = (yy - 2.0 * along * xy + along * along * xx) / norm_sq
    h12 = on_first
    h22 = 1.0 + on_second
    h32 = jnp.sqrt(jnp.maximum(length - on_first * on_first - on_second * on_second, 0.0))
    radius = jnp.sqrt(h11 * h11 + h21 * h21)
    cosine = h11 / radius
    sine = h21 / radius
    top = cosine * h12 + sine * h22
    low = -sine * h12 + cosine * h22
    target_top = cosine * beta
    target_low = -sine * beta
    second_radius = jnp.sqrt(low * low + h32 * h32)
    weight_two = (low / second_radius) * target_low / second_radius
    weight_one = (target_top - top * weight_two) / radius
    scale_two = weight_two / norm
    return weight_one / beta - scale_two * along, scale_two


def update_kernel(
    sz, sums_ref, guess_one, moves_one, guess_two, moves_two, update_ref,
):
    line = jnp.sum(sums_ref[...], axis=0)
    lane = iota((1, sz.nx), 1)
    gram = [
        jnp.sum(jnp.where(lane == no, line, 0.0), axis=1, keepdims=True) for no in range(6)
    ]
    one, two = weights_of(gram)
    for k in range(sz.lz):
        update_ref[0, k] = one * guess_one[k] + two * guess_two[k]
        update_ref[1, k] = one * moves_one[0, k] + two * moves_two[0, k]
        update_ref[2, k] = one * moves_one[1, k] + two * moves_two[1, k]


def call(kernel, sz, outs, *args):
    space = pl.BlockSpec(memory_space=pltpu.VMEM)
    return pl.pallas_call(
        functools.partial(kernel, sz),
        out_shape=[jax.ShapeDtypeStruct(shape, dtype) for shape, dtype in outs],
        in_specs=[space] * len(args),
        out_specs=[space] * len(outs),
        compiler_params=pltpu.CompilerParams(vmem_limit_bytes=16 * 2**20),
    )(*args)


def pair_swap(sz, value, first):
    pairs = []
    for low in range(first, sz.layer - 1, 2):
        pairs += [(low, low + 1), (low + 1, low)]
    return lax.ppermute(value, "layer", pairs)


def exchange(sz, send, even, odd):
    return (
        lax.all_to_all(send, "areal", split_axis=0, concat_axis=0, tiled=True),
        pair_swap(sz, even, 0),
        pair_swap(sz, odd, 1),
    )


def local(
    pressure,
    pressure_old,
    saturations,
    saturations_old,
    pore_volume,
    trans,
    upwind,
    active,
    fault_cell,
    fault_live,
    fault_up,
    fault_trans,
):
    sz = Sizes(
        lax.axis_size("areal"), lax.axis_size("layer"), pressure.shape, fault_cell.shape[3]
    )
    cells = pressure.shape

    def field(count):
        return ((count,) + cells, F32)

    def sends(y_fields, slot_fields, z_fields):
        return [
            ((sz.areal, sz.block_rows(y_fields, slot_fields), sz.nx), F32),
            ((z_fields, sz.ry, sz.nx), F32),
            ((z_fields, sz.ry, sz.nx), F32),
        ]

    one_field = sends(1, 1, 1)
    two_fields = sends(2, 2, 2)
    scalar = (cells, F32)
    *out, col_hot, row_hot, mine = call(
        pack_kernel,
        sz,
        sends(5, 4, 5)
        + [((sz.nx, sz.slots), BF16), ((sz.rows, sz.slots), F32), ((4, sz.slots), F32)],
        pressure, saturations, active, trans, upwind, fault_cell,
    )
    moved = exchange(sz, *out)
    resid, start, total_co, image_co, sat_co, inverse, slots, rhs, guess, *out = call(
        setup_kernel,
        sz,
        [field(3), field(3), field(6), field(21), field(22), field(3), ((10, sz.slots), F32),
         scalar, scalar] + one_field,
        *moved, pressure, pressure_old, saturations, saturations_old, pore_volume, trans, upwind,
        active, fault_live, fault_up, fault_trans, col_hot, row_hot, mine,
    )

    def precondition(vector, rhs, guess, out):
        for _ in range(SWEEPS - 1):
            moved = exchange(sz, *out)
            guess, *out = call(
                sweep_kernel, sz, [scalar] + one_field,
                *moved, guess, rhs, total_co, inverse, slots, col_hot, row_hot,
            )
        moved = exchange(sz, *out)
        image, moves, picked, *out = call(
            second_kernel, sz, [field(3), field(2), ((2, sz.slots), F32)] + two_fields,
            *moved, guess, vector, image_co, inverse, slots, col_hot, row_hot,
        )
        return guess, moves, picked, image, exchange(sz, *out)

    guess_one, moves_one, picked, image, moved = precondition(start, rhs, guess, out)
    shifted, rhs, guess, *out = call(
        next_kernel, sz, [field(3), scalar, scalar] + one_field,
        *moved, moves_one, picked, image, start, sat_co, inverse, slots, col_hot, row_hot,
    )
    guess_two, moves_two, picked, image, moved = precondition(shifted, rhs, guess, out)
    (sums,) = call(
        gram_kernel, sz, [((sz.areal * sz.layer, 1, sz.nx), F32)],
        *moved, moves_two, picked, image, start, shifted, sat_co, slots, col_hot, row_hot,
    )
    sums = lax.all_to_all(sums, ("areal", "layer"), split_axis=0, concat_axis=0, tiled=True)
    (update,) = call(
        update_kernel, sz, [field(3)], sums, guess_one, moves_one, guess_two, moves_two
    )
    return (resid, update)


def solution(mesh):
    cell = P("layer", "areal", None)
    rows = P(None, "layer", "areal", None)
    fault = P("layer", "areal", None, None)
    return jax.shard_map(
        local,
        mesh=mesh,
        in_specs=(cell, cell, rows, rows, cell, rows, rows, cell, fault, fault, fault, fault),
        out_specs=(rows, rows),
        check_vma=False,
    )
```

```python
import functools

import jax
import jax.numpy as jnp
from jax import lax
from jax.experimental import pallas as pl
from jax.experimental.pallas import tpu as pltpu
from jax.sharding import PartitionSpec as P

SWEEPS = 4

COMPRESS = (0.01, 0.02, 0.05)
DAMPING = 0.7

F32 = jnp.float32
BF16 = jnp.bfloat16


class Sizes:
    def __init__(self, areal, layer, cells, cap):
        self.areal = areal
        self.layer = layer
        self.lz, self.ry, self.nx = cells
        self.cap = cap
        self.rows = self.lz * self.ry
        self.slots = areal * cap

    def block_rows(self, y_fields, slot_fields):
        used = y_fields * self.lz + slot_fields
        return -(-used // 8) * 8


def iota(shape, dim):
    return lax.broadcasted_iota(jnp.int32, shape, dim)


def layers_of(sz, ref, *lead):
    return [ref[lead + (no,)] for no in range(sz.lz)]


def put_layers(ref, lead, parts):
    for no, part in enumerate(parts):
        ref[lead + (no,)] = part


def split_parts(value):
    high = value.astype(BF16)
    rest = value - high.astype(F32)
    middle = rest.astype(BF16)
    low = (rest - middle.astype(F32)).astype(BF16)
    return high, middle, low


def gather_slots(sz, fields, row_hot, col_hot):
    pieces = [split_parts(jnp.concatenate(field, axis=0)) for field in fields]
    lhs = jnp.concatenate([part for piece in pieces for part in piece], axis=0)
    picked = jnp.dot(lhs, col_hot, preferred_element_type=F32)
    out = []
    for no in range(len(fields)):
        base = 3 * no * sz.rows
        high = picked[base : base + sz.rows]
        middle = picked[base + sz.rows : base + 2 * sz.rows]
        low = picked[base + 2 * sz.rows : base + 3 * sz.rows]
        full = (low + middle) + high
        out.append(jnp.sum(full * row_hot, axis=0, keepdims=True))
    return jnp.concatenate(out, axis=0)


def scatter_slots(sz, values, row_hot, col_hot):
    count = values.shape[0]
    pieces = []
    for no in range(count):
        value = values[no : no + 1]
        high = value.astype(BF16).astype(F32)
        rest = value - high
        middle = rest.astype(BF16).astype(F32)
        low = (rest - middle).astype(BF16).astype(F32)
        for part in (high, middle, low):
            pieces.append((row_hot * part).astype(BF16))
    lhs = jnp.concatenate(pieces, axis=0)
    spread = lax.dot_general(
        lhs, col_hot, (((1,), (1,)), ((), ())), preferred_element_type=F32
    )
    out = []
    for no in range(count):
        base = 3 * no * sz.rows
        high = spread[base : base + sz.rows]
        middle = spread[base + sz.rows : base + 2 * sz.rows]
        low = spread[base + 2 * sz.rows : base + 3 * sz.rows]
        full = (low + middle) + high
        out.append([full[k * sz.ry : (k + 1) * sz.ry] for k in range(sz.lz)])
    return out


def lane_row(sz, ref):
    return jnp.concatenate([ref[0, 0, j : j + 1, :] for j in range(sz.areal)], axis=1)


def paired_lanes(sz):
    return 2 * sz.cap == sz.nx and sz.areal % 2 == 0


def read_slots(sz, recv_ref, first, count):
    blocks = [recv_ref[j, first : first + count, :] for j in range(sz.areal)]
    if not paired_lanes(sz):
        return jnp.concatenate([block[:, : sz.cap] for block in blocks], axis=1)
    left = iota((count, sz.nx), 1) < sz.cap
    return jnp.concatenate(
        [jnp.where(left, blocks[j], blocks[j + 1]) for j in range(0, sz.areal, 2)], axis=1
    )


def write_slots(sz, send_ref, first, values):
    count = values.shape[0]
    if not paired_lanes(sz):
        for j in range(sz.areal):
            part = values[:, j * sz.cap : (j + 1) * sz.cap]
            send_ref[j, first : first + count, 0 : sz.cap] = part
        return
    left = iota((count, sz.nx), 1) < sz.cap
    for j in range(0, sz.areal, 2):
        tile = values[:, j * sz.cap : (j + 2) * sz.cap]
        turned = pltpu.roll(tile, sz.cap, 1)
        send_ref[j, first : first + count, :] = jnp.where(left, tile, turned)
        send_ref[j + 1, first : first + count, :] = jnp.where(left, turned, tile)


def even_layer(sz):
    place = lax.rem(lax.axis_index("layer"), 2)
    return jnp.full((sz.ry, sz.nx), place, jnp.int32) == 0


def write_halo(sz, send_ref, even_ref, odd_ref, y_up, y_down, z_up, z_down):
    me = lax.axis_index("areal")

    @pl.when(me < sz.areal - 1)
    def _():
        for f, field in enumerate(y_up):
            for k in range(sz.lz):
                send_ref[me + 1, f * sz.lz + k : f * sz.lz + k + 1, :] = field[k][sz.ry - 1 : sz.ry]

    @pl.when(me > 0)
    def _():
        for f, field in enumerate(y_down):
            for k in range(sz.lz):
                send_ref[me - 1, f * sz.lz + k : f * sz.lz + k + 1, :] = field[k][0:1]

    even = even_layer(sz)
    for f in range(len(z_up)):
        top = z_up[f][sz.lz - 1]
        bottom = z_down[f][0] if f < len(z_down) else top
        even_ref[f] = jnp.where(even, top, bottom)
        odd_ref[f] = jnp.where(even, bottom, top)


def read_halo(sz, recv_ref, even_ref, odd_ref, low_fields, high_fields):
    me = lax.axis_index("areal")
    has_low = jnp.full((1, sz.nx), me, jnp.int32) > 0
    has_high = jnp.full((1, sz.nx), me, jnp.int32) < sz.areal - 1
    before = jnp.maximum(me - 1, 0)
    after = jnp.minimum(me + 1, sz.areal - 1)
    even = even_layer(sz)
    lows, highs = [], []
    for f in range(low_fields):
        y_part = [
            jnp.where(has_low, recv_ref[before, f * sz.lz + k : f * sz.lz + k + 1, :], 0.0)
            for k in range(sz.lz)
        ]
        lows.append((y_part, jnp.where(even, odd_ref[f], even_ref[f])))
    for f in range(high_fields):
        y_part = [
            jnp.where(has_high, recv_ref[after, f * sz.lz + k : f * sz.lz + k + 1, :], 0.0)
            for k in range(sz.lz)
        ]
        highs.append((y_part, jnp.where(even, even_ref[f], odd_ref[f])))
    return lows, highs


def x_below(sz, part):
    return pltpu.roll(part, 1, 1)


def x_above(sz, part):
    return pltpu.roll(part, sz.nx - 1, 1)


def y_below(sz, part, edge):
    return jnp.where(iota((sz.ry, sz.nx), 0) == 0, edge, pltpu.roll(part, 1, 0))


def y_above(sz, part, edge):
    return jnp.where(iota((sz.ry, sz.nx), 0) == sz.ry - 1, edge, pltpu.roll(part, sz.ry - 1, 0))


def neighbours(sz, field, k, low, high):
    below = field[k - 1] if k > 0 else low[1]
    above = field[k + 1] if k < sz.lz - 1 else high[1]
    return (
        x_below(sz, field[k]),
        x_above(sz, field[k]),
        y_below(sz, field[k], low[0][k]),
        y_above(sz, field[k], high[0][k]),
        below,
        above,
    )


def inner_neighbours(sz, field, k):
    return (
        x_below(sz, field[k]),
        x_above(sz, field[k]),
        y_below(sz, field[k], 0.0),
        y_above(sz, field[k], 0.0),
        field[k - 1] if k > 0 else None,
        field[k + 1] if k < sz.lz - 1 else None,
    )


def weighted(values, ref, lead):
    total = None
    for d, value in enumerate(values):
        if value is not None:
            term = ref[lead(d)] * value
            total = term if total is None else total + term
    return total


def edge_values(sz, k, low, high):
    row = iota((sz.ry, sz.nx), 0)
    return (
        None,
        None,
        jnp.where(row == 0, low[0][k], 0.0),
        jnp.where(row == sz.ry - 1, high[0][k], 0.0),
        low[1] if k == 0 else None,
        high[1] if k == sz.lz - 1 else None,
    )


def mobility(sat_water, sat_gas):
    sat_oil = 1.0 - sat_water - sat_gas
    mobile = (
        sat_water * sat_water * 2.0,
        sat_oil * sat_oil * 0.5,
        sat_gas * sat_gas * 5.0,
    )
    slopes = (4.0 * sat_water, -sat_oil, 10.0 * sat_gas)
    return mobile, slopes


def pack_kernel(
    sz, p_hbm, sat_hbm, act_hbm, trans_hbm, up_hbm, cell_hbm,
    send_hbm, even_ref, odd_ref, col_ref, row_ref, mine_ref,
    cell_ref, p_ref, sat_ref, act_ref, trans_ref, up_ref, send_ref, in_sems, sem,
):
    moves = [
        pltpu.make_async_copy(source, target, in_sems.at[no])
        for no, (source, target) in enumerate(
            (
                (cell_hbm, cell_ref),
                (p_hbm, p_ref),
                (sat_hbm, sat_ref),
                (act_hbm, act_ref),
                (trans_hbm.at[pl.ds(1, 2)], trans_ref),
                (up_hbm.at[pl.ds(1, 2)], up_ref),
            )
        )
    ]
    for move in moves:
        move.start()
    moves[0].wait()
    cell = lane_row(sz, cell_ref)
    row_start = iota((sz.rows, sz.slots), 0) * sz.nx
    in_row = (cell >= row_start) & (cell < row_start + sz.nx)
    row_hot = jnp.where(in_row, 1.0, 0.0)
    column = cell - jnp.sum(jnp.where(in_row, row_start, 0), axis=0, keepdims=True)
    col_hot = jnp.where(iota((sz.nx, sz.slots), 0) == column, 1.0, 0.0).astype(BF16)
    for move in moves[1:]:
        move.wait()
    pressure = layers_of(sz, p_ref)
    water = layers_of(sz, sat_ref, 0)
    gas = layers_of(sz, sat_ref, 1)
    act = [part.astype(F32) for part in layers_of(sz, act_ref)]
    four = [pressure, water, gas, act]
    mine = gather_slots(sz, four, row_hot, col_hot)
    write_slots(sz, send_ref, 5 * sz.lz, mine)
    ty = [t * a for t, a in zip(layers_of(sz, trans_ref, 0), act)]
    tz = [t * a for t, a in zip(layers_of(sz, trans_ref, 1), act)]
    uy = [u.astype(F32) for u in layers_of(sz, up_ref, 0)]
    uz = [u.astype(F32) for u in layers_of(sz, up_ref, 1)]
    write_halo(
        sz, send_ref, even_ref, odd_ref,
        [pressure, water, gas, ty, uy], four, [pressure, water, gas, tz, uz], four,
    )
    out = pltpu.make_async_copy(send_ref, send_hbm, sem)
    out.start()
    row_ref[...] = row_hot
    col_ref[...] = col_hot
    mine_ref[...] = mine
    out.wait()


def send_fields(sz, fields, row_hot, col_hot, send_hbm, even_ref, odd_ref, send_ref, sem):
    picked = gather_slots(sz, fields, row_hot, col_hot)
    write_halo(sz, send_ref, even_ref, odd_ref, fields, fields, fields, fields)
    write_slots(sz, send_ref, len(fields) * sz.lz, picked)
    out = pltpu.make_async_copy(send_ref, send_hbm, sem)
    out.start()
    return out, picked


def sweep_ready(sz, guesses, rhs, total_ref, relax, ready_ref):
    for k in range(sz.lz):
        total = weighted(inner_neighbours(sz, guesses, k), total_ref, lambda d: (d, k))
        ready_ref[k] = (1.0 - DAMPING) * guesses[k] + relax[k] * (rhs[k] + total)


def setup_kernel(
    sz, recv_ref, even_in, odd_in, p_ref, old_ref, sat_ref, sat_old_ref, pore_ref, trans_ref,
    up_ref, act_ref, live_ref, fup_ref, ftrans_ref, col_ref, row_ref, mine_ref,
    resid_hbm, start_ref, total_ref, image_ref, sat_co_ref, inv_ref, slot_ref,
    rhs_ref, ready_ref, send_hbm, even_ref, odd_ref, resid_ref, send_ref, sems,
):
    row_hot = row_ref[...]
    col_hot = col_ref[...]
    mine = mine_ref[...]
    their = read_slots(sz, recv_ref, 5 * sz.lz, 4)
    live = lane_row(sz, live_ref).astype(F32)
    high = lane_row(sz, fup_ref) > 0
    tau = lane_row(sz, ftrans_ref) * live * mine[3:4] * their[3:4]
    drop = their[0:1] - mine[0:1]
    mobile, slopes = mobility(
        jnp.where(high, their[1:2], mine[1:2]), jnp.where(high, their[2:3], mine[2:3])
    )
    flow = [tau * part for part in mobile]
    bend = [tau * drop * part for part in slopes]
    flow_sum = flow[0] + flow[1] + flow[2]
    scattered = scatter_slots(
        sz,
        jnp.concatenate(flow + [part * drop for part in flow], axis=0),
        row_hot,
        col_hot,
    )
    lows, highs = read_halo(sz, recv_ref, even_in, odd_in, 5, 4)
    pressure = layers_of(sz, p_ref)
    water = layers_of(sz, sat_ref, 0)
    gas = layers_of(sz, sat_ref, 1)
    act = [part.astype(F32) for part in layers_of(sz, act_ref)]
    trans = [layers_of(sz, trans_ref, axis) for axis in range(3)]
    flags = [[u.astype(F32) for u in layers_of(sz, up_ref, axis)] for axis in range(3)]
    carried = [[t * a for t, a in zip(trans[axis], act)] for axis in range(3)]
    lane = iota((sz.ry, sz.nx), 1)
    guesses, relaxes, rights = [], [], []
    for k in range(sz.lz):
        own_act = act[k]
        spare = 1.0 - own_act
        near = [
            neighbours(sz, field, k, lows[f], highs[f])
            for f, field in enumerate((pressure, water, gas, act))
        ]
        below_y = y_below(sz, carried[1][k], lows[3][0][k])
        flag_y = y_below(sz, flags[1][k], lows[4][0][k])
        below_z = carried[2][k - 1] if k > 0 else lows[3][1]
        flag_z = flags[2][k - 1] if k > 0 else lows[4][1]
        taus = (
            jnp.where(lane > 0, x_below(sz, carried[0][k]) * own_act, 0.0),
            jnp.where(lane < sz.nx - 1, carried[0][k] * near[3][1], 0.0),
            below_y * own_act,
            carried[1][k] * near[3][3],
            below_z * own_act,
            carried[2][k] * near[3][5],
        )
        other_up = (
            x_below(sz, flags[0][k]) < 0.5,
            flags[0][k] > 0.5,
            flag_y < 0.5,
            flags[1][k] > 0.5,
            flag_z < 0.5,
            flags[2][k] > 0.5,
        )
        change = pressure[k] - old_ref[k]
        oil = 1.0 - water[k] - gas[k]
        old_water = sat_old_ref[0, k]
        old_gas = sat_old_ref[1, k]
        now = (water[k], oil, gas[k])
        before = (old_water, 1.0 - old_water - old_gas, old_gas)
        pore = pore_ref[k]
        store_p = [own_act * pore * c * s for c, s in zip(COMPRESS, now)]
        store_s = [pore * (1.0 + c * change) for c in COMPRESS]
        resid = [
            own_act * (pore * (s - b + c * s * change)) for c, s, b in zip(COMPRESS, now, before)
        ]
        image_own = [store_p[0], store_p[1], store_p[2]]
        sat_own = [own_act * store_s[0], -(own_act * store_s[1]), own_act * store_s[2]]
        diag = store_p[0] + store_p[1] + store_p[2]
        for d in range(6):
            step = near[0][d] - pressure[k]
            mobile, slopes = mobility(
                jnp.where(other_up[d], near[1][d], water[k]),
                jnp.where(other_up[d], near[2][d], gas[k]),
            )
            face_flow = [taus[d] * part for part in mobile]
            total = face_flow[0] + face_flow[1] + face_flow[2]
            total_ref[d, k] = total
            diag = diag + total
            slope_tau = taus[d] * step
            for row in range(3):
                resid[row] = resid[row] - face_flow[row] * step
                image_own[row] = image_own[row] + face_flow[row]
                image_ref[3 + 6 * row + d, k] = face_flow[row]
                face_bend = slope_tau * slopes[row]
                sat_co_ref[4 + 6 * row + d, k] = jnp.where(other_up[d], face_bend, 0.0)
                sat_own[row] = sat_own[row] - jnp.where(other_up[d], 0.0, face_bend)
        for row in range(3):
            resid[row] = resid[row] - scattered[3 + row][k]
            image_own[row] = image_own[row] + scattered[row][k]
            resid_ref[row, k] = resid[row]
            start_ref[row, k] = -resid[row]
        diag = diag + (scattered[0][k] + scattered[1][k] + scattered[2][k]) + spare
        image_ref[0, k] = image_own[0] + spare
        image_ref[1, k] = image_own[1]
        image_ref[2, k] = image_own[2]
        sat_co_ref[0, k] = sat_own[0]
        sat_co_ref[1, k] = sat_own[1]
        sat_co_ref[2, k] = sat_own[2] + spare
        sat_co_ref[3, k] = spare
        relax = DAMPING / diag
        inv_ref[0, k] = relax
        inv_ref[1, k] = own_act / store_s[0]
        inv_ref[2, k] = own_act / store_s[2]
        rhs = -(resid[0] + resid[1] + resid[2])
        rhs_ref[k] = rhs
        relaxes.append(relax)
        rights.append(rhs)
        guesses.append(relax * rhs)
    resid_out = pltpu.make_async_copy(resid_ref, resid_hbm, sems.at[1])
    resid_out.start()
    out, _ = send_fields(
        sz, [guesses], row_hot, col_hot, send_hbm, even_ref, odd_ref, send_ref, sems.at[0]
    )
    slot_ref[...] = jnp.concatenate(
        [flow_sum]
        + flow
        + [jnp.where(high, 0.0, part) for part in bend]
        + [jnp.where(high, part, 0.0) for part in bend],
        axis=0,
    )
    sweep_ready(sz, guesses, rights, total_ref, relaxes, ready_ref)
    resid_out.wait()
    out.wait()


def next_guess(sz, recv_ref, even_in, odd_in, ready_in, total_ref, inv_ref, slot_ref, row_hot,
               col_hot):
    their = read_slots(sz, recv_ref, sz.lz, 1)
    scattered = scatter_slots(sz, slot_ref[0:1] * their, row_hot, col_hot)[0]
    lows, highs = read_halo(sz, recv_ref, even_in, odd_in, 1, 1)
    guesses = []
    for k in range(sz.lz):
        outside = weighted(edge_values(sz, k, lows[0], highs[0]), total_ref, lambda d: (d, k))
        guesses.append(ready_in[k] + inv_ref[0, k] * (outside + scattered[k]))
    return guesses


def sweep_kernel(
    sz, recv_ref, even_in, odd_in, ready_in, rhs_ref, total_ref, inv_ref, slot_ref, col_ref,
    row_ref, ready_ref, send_hbm, even_ref, odd_ref, send_ref, sem,
):
    row_hot = row_ref[...]
    col_hot = col_ref[...]
    guesses = next_guess(
        sz, recv_ref, even_in, odd_in, ready_in, total_ref, inv_ref, slot_ref, row_hot, col_hot
    )
    out, _ = send_fields(
        sz, [guesses], row_hot, col_hot, send_hbm, even_ref, odd_ref, send_ref, sem
    )
    sweep_ready(
        sz, guesses, layers_of(sz, rhs_ref), total_ref, layers_of(sz, inv_ref, 0), ready_ref
    )
    out.wait()


def last_sweep_kernel(
    sz, recv_ref, even_in, odd_in, ready_in, total_ref, inv_ref, image_co_ref, slot_ref, col_ref,
    row_ref, guess_ref, image_ref, send_hbm, even_ref, odd_ref, send_ref, sem,
):
    row_hot = row_ref[...]
    col_hot = col_ref[...]
    guesses = next_guess(
        sz, recv_ref, even_in, odd_in, ready_in, total_ref, inv_ref, slot_ref, row_hot, col_hot
    )
    out, _ = send_fields(
        sz, [guesses], row_hot, col_hot, send_hbm, even_ref, odd_ref, send_ref, sem
    )
    for k in range(sz.lz):
        guess_ref[k] = guesses[k]
        near = inner_neighbours(sz, guesses, k)
        for row in range(3):
            image_ref[row, k] = image_co_ref[row, k] * guesses[k] - weighted(
                near, image_co_ref, lambda d: (3 + 6 * row + d, k)
            )
    out.wait()


def second_kernel(
    sz, recv_ref, even_in, odd_in, image_in, vector_ref, image_co_ref, sat_co_ref, inv_ref,
    slot_ref, col_ref, row_ref, moves_ref, rows_ref, picked_ref, send_hbm, even_ref, odd_ref,
    send_ref, sem,
):
    row_hot = row_ref[...]
    col_hot = col_ref[...]
    their = read_slots(sz, recv_ref, sz.lz, 1)
    scattered = scatter_slots(sz, slot_ref[1:4] * their, row_hot, col_hot)
    lows, highs = read_halo(sz, recv_ref, even_in, odd_in, 1, 1)
    water, gas, images = [], [], []
    for k in range(sz.lz):
        outside = edge_values(sz, k, lows[0], highs[0])
        image = [
            image_in[row, k]
            - (
                weighted(outside, image_co_ref, lambda d: (3 + 6 * row + d, k))
                + scattered[row][k]
            )
            for row in range(3)
        ]
        images.append(image)
        water.append(inv_ref[1, k] * (vector_ref[0, k] - image[0]))
        gas.append(inv_ref[2, k] * (vector_ref[2, k] - image[2]))
    out, picked = send_fields(
        sz, [water, gas], row_hot, col_hot, send_hbm, even_ref, odd_ref, send_ref, sem
    )
    picked_ref[...] = picked
    both = [w + g for w, g in zip(water, gas)]
    for k in range(sz.lz):
        moves_ref[0, k] = water[k]
        moves_ref[1, k] = gas[k]
        own = (water[k], both[k], gas[k])
        near_w = inner_neighbours(sz, water, k)
        near_g = inner_neighbours(sz, gas, k)
        near = (near_w, [None if w is None else w + g for w, g in zip(near_w, near_g)], near_g)
        for row in range(3):
            value = images[k][row] + sat_co_ref[row, k] * own[row]
            if row == 1:
                value = value + sat_co_ref[3, k] * water[k]
            rows_ref[row, k] = value - weighted(
                near[row], sat_co_ref, lambda d: (4 + 6 * row + d, k)
            )
    out.wait()


def apply_sat(sz, recv_ref, even_in, odd_in, rows_in, picked_ref, co_ref, slot_ref, col_hot,
              row_hot):
    their = read_slots(sz, recv_ref, 2 * sz.lz, 2)
    mine = picked_ref[...]
    mine_rows = (mine[0:1], mine[0:1] + mine[1:2], mine[1:2])
    their_rows = (their[0:1], their[0:1] + their[1:2], their[1:2])
    values = jnp.concatenate(
        [
            slot_ref[4 + row : 5 + row] * mine_rows[row]
            + slot_ref[7 + row : 8 + row] * their_rows[row]
            for row in range(3)
        ],
        axis=0,
    )
    scattered = scatter_slots(sz, values, row_hot, col_hot)
    lows, highs = read_halo(sz, recv_ref, even_in, odd_in, 2, 2)
    rows = []
    for k in range(sz.lz):
        near_w = edge_values(sz, k, lows[0], highs[0])
        near_g = edge_values(sz, k, lows[1], highs[1])
        near = (near_w, [None if w is None else w + g for w, g in zip(near_w, near_g)], near_g)
        rows.append(
            [
                rows_in[row, k]
                - (
                    weighted(near[row], co_ref, lambda d: (4 + 6 * row + d, k))
                    + scattered[row][k]
                )
                for row in range(3)
            ]
        )
    return rows


def next_kernel(
    sz, recv_ref, even_in, odd_in, rows_in, picked_ref, vector_ref, sat_co_ref, total_ref, inv_ref,
    slot_ref, col_ref, row_ref, shifted_ref, rhs_ref, ready_ref, send_hbm, even_ref, odd_ref,
    send_ref, sem,
):
    row_hot = row_ref[...]
    col_hot = col_ref[...]
    rows = apply_sat(
        sz, recv_ref, even_in, odd_in, rows_in, picked_ref, sat_co_ref, slot_ref, col_hot, row_hot
    )
    guesses, rights, relaxes = [], [], []
    for k in range(sz.lz):
        shifted = [rows[k][row] - vector_ref[row, k] for row in range(3)]
        for row in range(3):
            shifted_ref[row, k] = shifted[row]
        rhs = shifted[0] + shifted[1] + shifted[2]
        rhs_ref[k] = rhs
        relax = inv_ref[0, k]
        rights.append(rhs)
        relaxes.append(relax)
        guesses.append(relax * rhs)
    out, _ = send_fields(
        sz, [guesses], row_hot, col_hot, send_hbm, even_ref, odd_ref, send_ref, sem
    )
    sweep_ready(sz, guesses, rights, total_ref, relaxes, ready_ref)
    out.wait()


def gram_kernel(
    sz, recv_ref, even_in, odd_in, rows_in, picked_ref, start_ref, vector_ref, co_ref, slot_ref,
    col_ref, row_ref, sums_ref,
):
    rows = apply_sat(
        sz, recv_ref, even_in, odd_in, rows_in, picked_ref, co_ref, slot_ref, col_ref[...],
        row_ref[...],
    )
    sums = [jnp.zeros((sz.ry, sz.nx), F32) for _ in range(6)]
    for k in range(sz.lz):
        for row in range(3):
            first = start_ref[row, k]
            second = vector_ref[row, k]
            third = rows[k][row] - second
            pairs = (
                (first, first), (first, second), (second, second),
                (first, third), (second, third), (third, third),
            )
            sums = [total + a * b for total, (a, b) in zip(sums, pairs)]
    lane = iota((1, sz.nx), 1)
    line = jnp.zeros((1, sz.nx), F32)
    for no, total in enumerate(sums):
        value = jnp.sum(jnp.sum(total, axis=0, keepdims=True), axis=1, keepdims=True)
        line = jnp.where(lane == no, value, line)
    sums_ref[...] = jnp.broadcast_to(line.reshape(1, 1, sz.nx), sums_ref.shape)


def weights_of(gram):
    rr, rx, xx, ry, xy, yy = gram
    beta = jnp.sqrt(rr)
    along = rx / rr
    norm_sq = jnp.maximum(xx - along * rx, 0.0)
    norm = jnp.sqrt(norm_sq)
    h11 = 1.0 + along
    h21 = norm / beta
    on_first = (ry - along * rx) / (norm * beta)
    on_second = (xy - along * xx - along * ry + along * along * rx) / norm_sq
    length = (yy - 2.0 * along * xy + along * along * xx) / norm_sq
    h12 = on_first
    h22 = 1.0 + on_second
    h32 = jnp.sqrt(jnp.maximum(length - on_first * on_first - on_second * on_second, 0.0))
    radius = jnp.sqrt(h11 * h11 + h21 * h21)
    cosine = h11 / radius
    sine = h21 / radius
    top = cosine * h12 + sine * h22
    low = -sine * h12 + cosine * h22
    target_top = cosine * beta
    target_low = -sine * beta
    second_radius = jnp.sqrt(low * low + h32 * h32)
    weight_two = (low / second_radius) * target_low / second_radius
    weight_one = (target_top - top * weight_two) / radius
    scale_two = weight_two / norm
    return weight_one / beta - scale_two * along, scale_two


def update_kernel(
    sz, sums_ref, guess_one, moves_one, guess_two, moves_two, update_ref,
):
    line = jnp.sum(sums_ref[...], axis=0)
    lane = iota((1, sz.nx), 1)
    gram = [
        jnp.sum(jnp.where(lane == no, line, 0.0), axis=1, keepdims=True) for no in range(6)
    ]
    one, two = weights_of(gram)
    for k in range(sz.lz):
        update_ref[0, k] = one * guess_one[k] + two * guess_two[k]
        update_ref[1, k] = one * moves_one[0, k] + two * moves_two[0, k]
        update_ref[2, k] = one * moves_one[1, k] + two * moves_two[1, k]


def call(kernel, sz, outs, *args, far_in=False, far_out=(), scratch=()):
    near = pl.BlockSpec(memory_space=pltpu.VMEM)
    far = pl.BlockSpec(memory_space=pltpu.HBM)
    return pl.pallas_call(
        functools.partial(kernel, sz),
        out_shape=[jax.ShapeDtypeStruct(shape, dtype) for shape, dtype in outs],
        in_specs=[far if far_in else near] * len(args),
        out_specs=[far if no in far_out else near for no in range(len(outs))],
        scratch_shapes=list(scratch),
        compiler_params=pltpu.CompilerParams(vmem_limit_bytes=16 * 2**20),
    )(*args)


def pair_swap(sz, value, first):
    pairs = []
    for low in range(first, sz.layer - 1, 2):
        pairs += [(low, low + 1), (low + 1, low)]
    return lax.ppermute(value, "layer", pairs)


def exchange(sz, send, even, odd):
    return (
        lax.all_to_all(send, "areal", split_axis=0, concat_axis=0, tiled=True),
        pair_swap(sz, even, 0),
        pair_swap(sz, odd, 1),
    )


def local(
    pressure,
    pressure_old,
    saturations,
    saturations_old,
    pore_volume,
    trans,
    upwind,
    active,
    fault_cell,
    fault_live,
    fault_up,
    fault_trans,
):
    sz = Sizes(
        lax.axis_size("areal"), lax.axis_size("layer"), pressure.shape, fault_cell.shape[3]
    )
    cells = pressure.shape

    def field(count):
        return ((count,) + cells, F32)

    def sends(y_fields, slot_fields, z_fields):
        return [
            ((sz.areal, sz.block_rows(y_fields, slot_fields), sz.nx), F32),
            ((z_fields, sz.ry, sz.nx), F32),
            ((z_fields, sz.ry, sz.nx), F32),
        ]

    def sender(kernel, outs, to_send, *args):
        buffers = [pltpu.VMEM(*to_send[0]), pltpu.SemaphoreType.DMA]
        *kept, send, even, odd = call(
            kernel, sz, outs + to_send, *args, far_out=(len(outs),), scratch=buffers
        )
        return *kept, exchange(sz, send, even, odd)

    one_field = sends(1, 1, 1)
    two_fields = sends(2, 2, 2)
    state = sends(5, 4, 5)
    scalar = (cells, F32)
    *out, col_hot, row_hot, mine = call(
        pack_kernel,
        sz,
        state + [((sz.nx, sz.slots), BF16), ((sz.rows, sz.slots), F32), ((4, sz.slots), F32)],
        pressure, saturations, active, trans, upwind, fault_cell,
        far_in=True,
        far_out=(0,),
        scratch=[
            pltpu.VMEM(fault_cell.shape, jnp.int32),
            pltpu.VMEM(cells, F32),
            pltpu.VMEM((2,) + cells, F32),
            pltpu.VMEM(cells, jnp.int32),
            pltpu.VMEM((2,) + cells, F32),
            pltpu.VMEM((2,) + cells, jnp.int32),
            pltpu.VMEM(*state[0]),
            pltpu.SemaphoreType.DMA((6,)),
            pltpu.SemaphoreType.DMA,
        ],
    )
    moved = exchange(sz, *out)
    resid, start, total_co, image_co, sat_co, inverse, slots, rhs, ready, *out = call(
        setup_kernel,
        sz,
        [field(3), field(3), field(6), field(21), field(22), field(3), ((10, sz.slots), F32),
         scalar, scalar] + one_field,
        *moved, pressure, pressure_old, saturations, saturations_old, pore_volume, trans, upwind,
        active, fault_live, fault_up, fault_trans, col_hot, row_hot, mine,
        far_out=(0, 9),
        scratch=[
            pltpu.VMEM(*field(3)), pltpu.VMEM(*one_field[0]), pltpu.SemaphoreType.DMA((2,))
        ],
    )
    moved = exchange(sz, *out)

    def precondition(vector, rhs, ready, moved):
        for _ in range(SWEEPS - 2):
            ready, moved = sender(
                sweep_kernel, [scalar], one_field,
                *moved, ready, rhs, total_co, inverse, slots, col_hot, row_hot,
            )
        guess, image, moved = sender(
            last_sweep_kernel, [scalar, field(3)], one_field,
            *moved, ready, total_co, inverse, image_co, slots, col_hot, row_hot,
        )
        moves, rows, picked, moved = sender(
            second_kernel, [field(2), field(3), ((2, sz.slots), F32)], two_fields,
            *moved, image, vector, image_co, sat_co, inverse, slots, col_hot, row_hot,
        )
        return guess, moves, rows, picked, moved

    guess_one, moves_one, rows, picked, moved = precondition(start, rhs, ready, moved)
    shifted, rhs, ready, moved = sender(
        next_kernel, [field(3), scalar, scalar], one_field,
        *moved, rows, picked, start, sat_co, total_co, inverse, slots, col_hot, row_hot,
    )
    guess_two, moves_two, rows, picked, moved = precondition(shifted, rhs, ready, moved)
    (sums,) = call(
        gram_kernel, sz, [((sz.areal * sz.layer, 1, sz.nx), F32)],
        *moved, rows, picked, start, shifted, sat_co, slots, col_hot, row_hot,
    )
    sums = lax.all_to_all(sums, ("areal", "layer"), split_axis=0, concat_axis=0, tiled=True)
    (update,) = call(
        update_kernel, sz, [field(3)], sums, guess_one, moves_one, guess_two, moves_two
    )
    return (resid, update)


def solution(mesh):
    cell = P("layer", "areal", None)
    rows = P(None, "layer", "areal", None)
    fault = P("layer", "areal", None, None)
    return jax.shard_map(
        local,
        mesh=mesh,
        in_specs=(cell, cell, rows, rows, cell, rows, rows, cell, fault, fault, fault, fault),
        out_specs=(rows, rows),
        check_vma=False,
    )
```

```python
import functools

import jax
import jax.numpy as jnp
from jax import lax
from jax.experimental import pallas as pl
from jax.experimental.pallas import tpu as pltpu
from jax.sharding import PartitionSpec as P

SWEEPS = 4

COMPRESS = (0.01, 0.02, 0.05)
DAMPING = 0.7

F32 = jnp.float32
BF16 = jnp.bfloat16


class Sizes:
    def __init__(self, areal, layer, cells, cap):
        self.areal = areal
        self.layer = layer
        self.lz, self.ry, self.nx = cells
        self.cap = cap
        self.rows = self.lz * self.ry
        self.slots = areal * cap

    def block_rows(self, y_fields, slot_fields):
        used = y_fields * self.lz + slot_fields
        return -(-used // 8) * 8


def iota(shape, dim):
    return lax.broadcasted_iota(jnp.int32, shape, dim)


def layers_of(sz, ref, *lead):
    return [ref[lead + (no,)] for no in range(sz.lz)]


def put_layers(ref, lead, parts):
    for no, part in enumerate(parts):
        ref[lead + (no,)] = part


def split_parts(value):
    high = value.astype(BF16)
    rest = value - high.astype(F32)
    middle = rest.astype(BF16)
    low = (rest - middle.astype(F32)).astype(BF16)
    return high, middle, low


def gather_slots(sz, fields, row_hot, col_hot):
    pieces = [split_parts(jnp.concatenate(field, axis=0)) for field in fields]
    lhs = jnp.concatenate([part for piece in pieces for part in piece], axis=0)
    picked = jnp.dot(lhs, col_hot, preferred_element_type=F32)
    out = []
    for no in range(len(fields)):
        base = 3 * no * sz.rows
        high = picked[base : base + sz.rows]
        middle = picked[base + sz.rows : base + 2 * sz.rows]
        low = picked[base + 2 * sz.rows : base + 3 * sz.rows]
        full = (low + middle) + high
        out.append(jnp.sum(full * row_hot, axis=0, keepdims=True))
    return jnp.concatenate(out, axis=0)


def scatter_slots(sz, values, row_hot, col_hot):
    count = values.shape[0]
    pieces = []
    for no in range(count):
        value = values[no : no + 1]
        high = value.astype(BF16).astype(F32)
        rest = value - high
        middle = rest.astype(BF16).astype(F32)
        low = (rest - middle).astype(BF16).astype(F32)
        for part in (high, middle, low):
            pieces.append((row_hot * part).astype(BF16))
    lhs = jnp.concatenate(pieces, axis=0)
    spread = lax.dot_general(
        lhs, col_hot, (((1,), (1,)), ((), ())), preferred_element_type=F32
    )
    out = []
    for no in range(count):
        base = 3 * no * sz.rows
        high = spread[base : base + sz.rows]
        middle = spread[base + sz.rows : base + 2 * sz.rows]
        low = spread[base + 2 * sz.rows : base + 3 * sz.rows]
        full = (low + middle) + high
        out.append([full[k * sz.ry : (k + 1) * sz.ry] for k in range(sz.lz)])
    return out


def lane_row(sz, ref):
    return jnp.concatenate([ref[0, 0, j : j + 1, :] for j in range(sz.areal)], axis=1)


def paired_lanes(sz):
    return 2 * sz.cap == sz.nx and sz.areal % 2 == 0


def read_slots(sz, recv_ref, first, count):
    blocks = [recv_ref[j, first : first + count, :] for j in range(sz.areal)]
    if not paired_lanes(sz):
        return jnp.concatenate([block[:, : sz.cap] for block in blocks], axis=1)
    left = iota((count, sz.nx), 1) < sz.cap
    return jnp.concatenate(
        [jnp.where(left, blocks[j], blocks[j + 1]) for j in range(0, sz.areal, 2)], axis=1
    )


def write_slots(sz, send_ref, first, values):
    count = values.shape[0]
    if not paired_lanes(sz):
        for j in range(sz.areal):
            part = values[:, j * sz.cap : (j + 1) * sz.cap]
            send_ref[j, first : first + count, 0 : sz.cap] = part
        return
    left = iota((count, sz.nx), 1) < sz.cap
    for j in range(0, sz.areal, 2):
        tile = values[:, j * sz.cap : (j + 2) * sz.cap]
        turned = pltpu.roll(tile, sz.cap, 1)
        send_ref[j, first : first + count, :] = jnp.where(left, tile, turned)
        send_ref[j + 1, first : first + count, :] = jnp.where(left, turned, tile)


def even_layer(sz):
    place = lax.rem(lax.axis_index("layer"), 2)
    return jnp.full((sz.ry, sz.nx), place, jnp.int32) == 0


def write_halo(sz, send_ref, even_ref, odd_ref, y_up, y_down, z_up, z_down):
    me = lax.axis_index("areal")

    @pl.when(me < sz.areal - 1)
    def _():
        for f, field in enumerate(y_up):
            for k in range(sz.lz):
                send_ref[me + 1, f * sz.lz + k : f * sz.lz + k + 1, :] = field[k][sz.ry - 1 : sz.ry]

    @pl.when(me > 0)
    def _():
        for f, field in enumerate(y_down):
            for k in range(sz.lz):
                send_ref[me - 1, f * sz.lz + k : f * sz.lz + k + 1, :] = field[k][0:1]

    even = even_layer(sz)
    for f in range(len(z_up)):
        top = z_up[f][sz.lz - 1]
        bottom = z_down[f][0] if f < len(z_down) else top
        even_ref[f] = jnp.where(even, top, bottom)
        odd_ref[f] = jnp.where(even, bottom, top)


def read_halo(sz, recv_ref, even_ref, odd_ref, low_fields, high_fields):
    me = lax.axis_index("areal")
    has_low = jnp.full((1, sz.nx), me, jnp.int32) > 0
    has_high = jnp.full((1, sz.nx), me, jnp.int32) < sz.areal - 1
    before = jnp.maximum(me - 1, 0)
    after = jnp.minimum(me + 1, sz.areal - 1)
    even = even_layer(sz)
    lows, highs = [], []
    for f in range(low_fields):
        y_part = [
            jnp.where(has_low, recv_ref[before, f * sz.lz + k : f * sz.lz + k + 1, :], 0.0)
            for k in range(sz.lz)
        ]
        lows.append((y_part, jnp.where(even, odd_ref[f], even_ref[f])))
    for f in range(high_fields):
        y_part = [
            jnp.where(has_high, recv_ref[after, f * sz.lz + k : f * sz.lz + k + 1, :], 0.0)
            for k in range(sz.lz)
        ]
        highs.append((y_part, jnp.where(even, even_ref[f], odd_ref[f])))
    return lows, highs


def x_below(sz, part):
    return pltpu.roll(part, 1, 1)


def x_above(sz, part):
    return pltpu.roll(part, sz.nx - 1, 1)


def y_below(sz, part, edge):
    return jnp.where(iota((sz.ry, sz.nx), 0) == 0, edge, pltpu.roll(part, 1, 0))


def y_above(sz, part, edge):
    return jnp.where(iota((sz.ry, sz.nx), 0) == sz.ry - 1, edge, pltpu.roll(part, sz.ry - 1, 0))


def neighbours(sz, field, k, low, high):
    below = field[k - 1] if k > 0 else low[1]
    above = field[k + 1] if k < sz.lz - 1 else high[1]
    return (
        x_below(sz, field[k]),
        x_above(sz, field[k]),
        y_below(sz, field[k], low[0][k]),
        y_above(sz, field[k], high[0][k]),
        below,
        above,
    )


def inner_neighbours(sz, field, k):
    return (
        x_below(sz, field[k]),
        x_above(sz, field[k]),
        y_below(sz, field[k], 0.0),
        y_above(sz, field[k], 0.0),
        field[k - 1] if k > 0 else None,
        field[k + 1] if k < sz.lz - 1 else None,
    )


def weighted(values, ref, lead):
    total = None
    for d, value in enumerate(values):
        if value is not None:
            term = ref[lead(d)] * value
            total = term if total is None else total + term
    return total


def edge_values(sz, k, low, high):
    row = iota((sz.ry, sz.nx), 0)
    return (
        None,
        None,
        jnp.where(row == 0, low[0][k], 0.0),
        jnp.where(row == sz.ry - 1, high[0][k], 0.0),
        low[1] if k == 0 else None,
        high[1] if k == sz.lz - 1 else None,
    )


def mobility(sat_water, sat_gas):
    sat_oil = 1.0 - sat_water - sat_gas
    mobile = (
        sat_water * sat_water * 2.0,
        sat_oil * sat_oil * 0.5,
        sat_gas * sat_gas * 5.0,
    )
    slopes = (4.0 * sat_water, -sat_oil, 10.0 * sat_gas)
    return mobile, slopes


def pack_kernel(
    sz, state_ref, cell_in,
    send_hbm, even_ref, odd_ref, col_ref, row_ref, mine_ref, send_ref, sem,
):
    cell = lane_row(sz, cell_in)
    row_start = iota((sz.rows, sz.slots), 0) * sz.nx
    in_row = (cell >= row_start) & (cell < row_start + sz.nx)
    row_hot = jnp.where(in_row, 1.0, 0.0)
    column = cell - jnp.sum(jnp.where(in_row, row_start, 0), axis=0, keepdims=True)
    col_hot = jnp.where(iota((sz.nx, sz.slots), 0) == column, 1.0, 0.0).astype(BF16)
    pressure, water, gas, act, _, ty, tz, _, uy, uz = [
        layers_of(sz, state_ref, no) for no in range(10)
    ]
    four = [pressure, water, gas, act]
    mine = gather_slots(sz, four, row_hot, col_hot)
    write_slots(sz, send_ref, 5 * sz.lz, mine)
    write_halo(
        sz, send_ref, even_ref, odd_ref,
        [pressure, water, gas, ty, uy], four, [pressure, water, gas, tz, uz], four,
    )
    out = pltpu.make_async_copy(send_ref, send_hbm, sem)
    out.start()

    @meanwhile
    def _():
        row_ref[...] = row_hot
        col_ref[...] = col_hot
        mine_ref[...] = mine

    out.wait()


def send_fields(sz, fields, row_hot, col_hot, send_hbm, even_ref, odd_ref, send_ref, sem):
    picked = gather_slots(sz, fields, row_hot, col_hot)
    write_halo(sz, send_ref, even_ref, odd_ref, fields, fields, fields, fields)
    write_slots(sz, send_ref, len(fields) * sz.lz, picked)
    out = pltpu.make_async_copy(send_ref, send_hbm, sem)
    out.start()
    return out, picked


def meanwhile(body):
    pl.when(lax.axis_index("areal") >= 0)(body)


def sweep_ready(sz, guesses, rhs, total_ref, relax, ready_ref):
    for k in range(sz.lz):
        total = weighted(inner_neighbours(sz, guesses, k), total_ref, lambda d: (d, k))
        ready_ref[k] = (1.0 - DAMPING) * guesses[k] + relax[k] * (rhs[k] + total)


def setup_kernel(
    sz, recv_ref, even_in, odd_in, state_ref, old_ref, sat_old_ref, pore_ref,
    live_ref, fup_ref, ftrans_ref, col_ref, row_ref, mine_ref,
    resid_hbm, start_ref, total_ref, image_ref, sat_co_ref, inv_ref, slot_ref,
    rhs_ref, ready_ref, send_hbm, even_ref, odd_ref, resid_ref, send_ref, sems,
):
    row_hot = row_ref[...]
    col_hot = col_ref[...]
    mine = mine_ref[...]
    their = read_slots(sz, recv_ref, 5 * sz.lz, 4)
    live = lane_row(sz, live_ref).astype(F32)
    high = lane_row(sz, fup_ref) > 0
    tau = lane_row(sz, ftrans_ref) * live * mine[3:4] * their[3:4]
    drop = their[0:1] - mine[0:1]
    mobile, slopes = mobility(
        jnp.where(high, their[1:2], mine[1:2]), jnp.where(high, their[2:3], mine[2:3])
    )
    flow = [tau * part for part in mobile]
    bend = [tau * drop * part for part in slopes]
    flow_sum = flow[0] + flow[1] + flow[2]
    scattered = scatter_slots(
        sz,
        jnp.concatenate(flow + [part * drop for part in flow], axis=0),
        row_hot,
        col_hot,
    )
    lows, highs = read_halo(sz, recv_ref, even_in, odd_in, 5, 4)
    pressure, water, gas, act, *faces = [layers_of(sz, state_ref, no) for no in range(10)]
    carried, flags = faces[:3], faces[3:]
    lane = iota((sz.ry, sz.nx), 1)
    guesses, relaxes, rights = [], [], []
    for k in range(sz.lz):
        own_act = act[k]
        spare = 1.0 - own_act
        near = [
            neighbours(sz, field, k, lows[f], highs[f])
            for f, field in enumerate((pressure, water, gas, act))
        ]
        below_y = y_below(sz, carried[1][k], lows[3][0][k])
        flag_y = y_below(sz, flags[1][k], lows[4][0][k])
        below_z = carried[2][k - 1] if k > 0 else lows[3][1]
        flag_z = flags[2][k - 1] if k > 0 else lows[4][1]
        taus = (
            jnp.where(lane > 0, x_below(sz, carried[0][k]) * own_act, 0.0),
            jnp.where(lane < sz.nx - 1, carried[0][k] * near[3][1], 0.0),
            below_y * own_act,
            carried[1][k] * near[3][3],
            below_z * own_act,
            carried[2][k] * near[3][5],
        )
        other_up = (
            x_below(sz, flags[0][k]) < 0.5,
            flags[0][k] > 0.5,
            flag_y < 0.5,
            flags[1][k] > 0.5,
            flag_z < 0.5,
            flags[2][k] > 0.5,
        )
        change = pressure[k] - old_ref[k]
        oil = 1.0 - water[k] - gas[k]
        old_water = sat_old_ref[0, k]
        old_gas = sat_old_ref[1, k]
        now = (water[k], oil, gas[k])
        before = (old_water, 1.0 - old_water - old_gas, old_gas)
        pore = pore_ref[k]
        store_p = [own_act * pore * c * s for c, s in zip(COMPRESS, now)]
        store_s = [pore * (1.0 + c * change) for c in COMPRESS]
        resid = [
            own_act * (pore * (s - b + c * s * change)) for c, s, b in zip(COMPRESS, now, before)
        ]
        image_own = [store_p[0], store_p[1], store_p[2]]
        sat_own = [own_act * store_s[0], -(own_act * store_s[1]), own_act * store_s[2]]
        diag = store_p[0] + store_p[1] + store_p[2]
        for d in range(6):
            step = near[0][d] - pressure[k]
            mobile, slopes = mobility(
                jnp.where(other_up[d], near[1][d], water[k]),
                jnp.where(other_up[d], near[2][d], gas[k]),
            )
            face_flow = [taus[d] * part for part in mobile]
            total = face_flow[0] + face_flow[1] + face_flow[2]
            total_ref[d, k] = total
            diag = diag + total
            slope_tau = taus[d] * step
            for row in range(3):
                resid[row] = resid[row] - face_flow[row] * step
                image_own[row] = image_own[row] + face_flow[row]
                image_ref[3 + 6 * row + d, k] = face_flow[row]
                face_bend = slope_tau * slopes[row]
                sat_co_ref[4 + 6 * row + d, k] = jnp.where(other_up[d], face_bend, 0.0)
                sat_own[row] = sat_own[row] - jnp.where(other_up[d], 0.0, face_bend)
        for row in range(3):
            resid[row] = resid[row] - scattered[3 + row][k]
            image_own[row] = image_own[row] + scattered[row][k]
            resid_ref[row, k] = resid[row]
            start_ref[row, k] = -resid[row]
        diag = diag + (scattered[0][k] + scattered[1][k] + scattered[2][k]) + spare
        image_ref[0, k] = image_own[0] + spare
        image_ref[1, k] = image_own[1]
        image_ref[2, k] = image_own[2]
        sat_co_ref[0, k] = sat_own[0]
        sat_co_ref[1, k] = sat_own[1]
        sat_co_ref[2, k] = sat_own[2] + spare
        sat_co_ref[3, k] = spare
        relax = DAMPING / diag
        inv_ref[0, k] = relax
        inv_ref[1, k] = own_act / store_s[0]
        inv_ref[2, k] = own_act / store_s[2]
        rhs = -(resid[0] + resid[1] + resid[2])
        rhs_ref[k] = rhs
        relaxes.append(relax)
        rights.append(rhs)
        guesses.append(relax * rhs)
    resid_out = pltpu.make_async_copy(resid_ref, resid_hbm, sems.at[1])
    resid_out.start()
    out, _ = send_fields(
        sz, [guesses], row_hot, col_hot, send_hbm, even_ref, odd_ref, send_ref, sems.at[0]
    )

    @meanwhile
    def _():
        slot_ref[...] = jnp.concatenate(
            [flow_sum]
            + flow
            + [jnp.where(high, 0.0, part) for part in bend]
            + [jnp.where(high, part, 0.0) for part in bend],
            axis=0,
        )
        sweep_ready(sz, guesses, rights, total_ref, relaxes, ready_ref)

    resid_out.wait()
    out.wait()


def next_guess(sz, recv_ref, even_in, odd_in, ready_in, total_ref, inv_ref, slot_ref, row_hot,
               col_hot):
    their = read_slots(sz, recv_ref, sz.lz, 1)
    scattered = scatter_slots(sz, slot_ref[0:1] * their, row_hot, col_hot)[0]
    lows, highs = read_halo(sz, recv_ref, even_in, odd_in, 1, 1)
    guesses = []
    for k in range(sz.lz):
        outside = weighted(edge_values(sz, k, lows[0], highs[0]), total_ref, lambda d: (d, k))
        guesses.append(ready_in[k] + inv_ref[0, k] * (outside + scattered[k]))
    return guesses


def sweep_kernel(
    sz, recv_ref, even_in, odd_in, ready_in, rhs_ref, total_ref, inv_ref, slot_ref, col_ref,
    row_ref, ready_ref, send_hbm, even_ref, odd_ref, send_ref, sem,
):
    row_hot = row_ref[...]
    col_hot = col_ref[...]
    guesses = next_guess(
        sz, recv_ref, even_in, odd_in, ready_in, total_ref, inv_ref, slot_ref, row_hot, col_hot
    )
    out, _ = send_fields(
        sz, [guesses], row_hot, col_hot, send_hbm, even_ref, odd_ref, send_ref, sem
    )

    @meanwhile
    def _():
        sweep_ready(
            sz, guesses, layers_of(sz, rhs_ref), total_ref, layers_of(sz, inv_ref, 0), ready_ref
        )

    out.wait()


def last_sweep_kernel(
    sz, recv_ref, even_in, odd_in, ready_in, total_ref, inv_ref, image_co_ref, slot_ref, col_ref,
    row_ref, guess_ref, image_ref, send_hbm, even_ref, odd_ref, send_ref, sem,
):
    row_hot = row_ref[...]
    col_hot = col_ref[...]
    guesses = next_guess(
        sz, recv_ref, even_in, odd_in, ready_in, total_ref, inv_ref, slot_ref, row_hot, col_hot
    )
    out, _ = send_fields(
        sz, [guesses], row_hot, col_hot, send_hbm, even_ref, odd_ref, send_ref, sem
    )

    @meanwhile
    def _():
        for k in range(sz.lz):
            guess_ref[k] = guesses[k]
            near = inner_neighbours(sz, guesses, k)
            for row in range(3):
                image_ref[row, k] = image_co_ref[row, k] * guesses[k] - weighted(
                    near, image_co_ref, lambda d: (3 + 6 * row + d, k)
                )

    out.wait()


def second_kernel(
    sz, recv_ref, even_in, odd_in, image_in, vector_ref, image_co_ref, sat_co_ref, inv_ref,
    slot_ref, col_ref, row_ref, moves_ref, rows_ref, picked_ref, send_hbm, even_ref, odd_ref,
    send_ref, sem,
):
    row_hot = row_ref[...]
    col_hot = col_ref[...]
    their = read_slots(sz, recv_ref, sz.lz, 1)
    scattered = scatter_slots(sz, slot_ref[1:4] * their, row_hot, col_hot)
    lows, highs = read_halo(sz, recv_ref, even_in, odd_in, 1, 1)
    water, gas, images = [], [], []
    for k in range(sz.lz):
        outside = edge_values(sz, k, lows[0], highs[0])
        image = [
            image_in[row, k]
            - (
                weighted(outside, image_co_ref, lambda d: (3 + 6 * row + d, k))
                + scattered[row][k]
            )
            for row in range(3)
        ]
        images.append(image)
        water.append(inv_ref[1, k] * (vector_ref[0, k] - image[0]))
        gas.append(inv_ref[2, k] * (vector_ref[2, k] - image[2]))
    out, picked = send_fields(
        sz, [water, gas], row_hot, col_hot, send_hbm, even_ref, odd_ref, send_ref, sem
    )

    @meanwhile
    def _():
        picked_ref[...] = picked
        both = [w + g for w, g in zip(water, gas)]
        for k in range(sz.lz):
            moves_ref[0, k] = water[k]
            moves_ref[1, k] = gas[k]
            own = (water[k], both[k], gas[k])
            near_w = inner_neighbours(sz, water, k)
            near_g = inner_neighbours(sz, gas, k)
            near = (near_w, [None if w is None else w + g for w, g in zip(near_w, near_g)], near_g)
            for row in range(3):
                value = images[k][row] + sat_co_ref[row, k] * own[row]
                if row == 1:
                    value = value + sat_co_ref[3, k] * water[k]
                rows_ref[row, k] = value - weighted(
                    near[row], sat_co_ref, lambda d: (4 + 6 * row + d, k)
                )

    out.wait()


def apply_sat(sz, recv_ref, even_in, odd_in, rows_in, picked_ref, co_ref, slot_ref, col_hot,
              row_hot):
    their = read_slots(sz, recv_ref, 2 * sz.lz, 2)
    mine = picked_ref[...]
    mine_rows = (mine[0:1], mine[0:1] + mine[1:2], mine[1:2])
    their_rows = (their[0:1], their[0:1] + their[1:2], their[1:2])
    values = jnp.concatenate(
        [
            slot_ref[4 + row : 5 + row] * mine_rows[row]
            + slot_ref[7 + row : 8 + row] * their_rows[row]
            for row in range(3)
        ],
        axis=0,
    )
    scattered = scatter_slots(sz, values, row_hot, col_hot)
    lows, highs = read_halo(sz, recv_ref, even_in, odd_in, 2, 2)
    rows = []
    for k in range(sz.lz):
        near_w = edge_values(sz, k, lows[0], highs[0])
        near_g = edge_values(sz, k, lows[1], highs[1])
        near = (near_w, [None if w is None else w + g for w, g in zip(near_w, near_g)], near_g)
        rows.append(
            [
                rows_in[row, k]
                - (
                    weighted(near[row], co_ref, lambda d: (4 + 6 * row + d, k))
                    + scattered[row][k]
                )
                for row in range(3)
            ]
        )
    return rows


def next_kernel(
    sz, recv_ref, even_in, odd_in, rows_in, picked_ref, vector_ref, sat_co_ref, total_ref, inv_ref,
    slot_ref, col_ref, row_ref, shifted_ref, rhs_ref, ready_ref, send_hbm, even_ref, odd_ref,
    send_ref, sem,
):
    row_hot = row_ref[...]
    col_hot = col_ref[...]
    rows = apply_sat(
        sz, recv_ref, even_in, odd_in, rows_in, picked_ref, sat_co_ref, slot_ref, col_hot, row_hot
    )
    guesses, rights, relaxes = [], [], []
    for k in range(sz.lz):
        shifted = [rows[k][row] - vector_ref[row, k] for row in range(3)]
        for row in range(3):
            shifted_ref[row, k] = shifted[row]
        rhs = shifted[0] + shifted[1] + shifted[2]
        rhs_ref[k] = rhs
        relax = inv_ref[0, k]
        rights.append(rhs)
        relaxes.append(relax)
        guesses.append(relax * rhs)
    out, _ = send_fields(
        sz, [guesses], row_hot, col_hot, send_hbm, even_ref, odd_ref, send_ref, sem
    )

    @meanwhile
    def _():
        sweep_ready(sz, guesses, rights, total_ref, relaxes, ready_ref)

    out.wait()


def gram_kernel(
    sz, recv_ref, even_in, odd_in, rows_in, picked_ref, start_ref, vector_ref, co_ref, slot_ref,
    col_ref, row_ref, sums_ref,
):
    rows = apply_sat(
        sz, recv_ref, even_in, odd_in, rows_in, picked_ref, co_ref, slot_ref, col_ref[...],
        row_ref[...],
    )
    sums = [jnp.zeros((sz.ry, sz.nx), F32) for _ in range(6)]
    for k in range(sz.lz):
        for row in range(3):
            first = start_ref[row, k]
            second = vector_ref[row, k]
            third = rows[k][row] - second
            pairs = (
                (first, first), (first, second), (second, second),
                (first, third), (second, third), (third, third),
            )
            sums = [total + a * b for total, (a, b) in zip(sums, pairs)]
    lane = iota((1, sz.nx), 1)
    line = jnp.zeros((1, sz.nx), F32)
    for no, total in enumerate(sums):
        value = jnp.sum(jnp.sum(total, axis=0, keepdims=True), axis=1, keepdims=True)
        line = jnp.where(lane == no, value, line)
    sums_ref[...] = jnp.broadcast_to(line.reshape(1, 1, sz.nx), sums_ref.shape)


def weights_of(gram):
    rr, rx, xx, ry, xy, yy = gram
    beta = jnp.sqrt(rr)
    along = rx / rr
    norm_sq = jnp.maximum(xx - along * rx, 0.0)
    norm = jnp.sqrt(norm_sq)
    h11 = 1.0 + along
    h21 = norm / beta
    on_first = (ry - along * rx) / (norm * beta)
    on_second = (xy - along * xx - along * ry + along * along * rx) / norm_sq
    length = (yy - 2.0 * along * xy + along * along * xx) / norm_sq
    h12 = on_first
    h22 = 1.0 + on_second
    h32 = jnp.sqrt(jnp.maximum(length - on_first * on_first - on_second * on_second, 0.0))
    radius = jnp.sqrt(h11 * h11 + h21 * h21)
    cosine = h11 / radius
    sine = h21 / radius
    top = cosine * h12 + sine * h22
    low = -sine * h12 + cosine * h22
    target_top = cosine * beta
    target_low = -sine * beta
    second_radius = jnp.sqrt(low * low + h32 * h32)
    weight_two = (low / second_radius) * target_low / second_radius
    weight_one = (target_top - top * weight_two) / radius
    scale_two = weight_two / norm
    return weight_one / beta - scale_two * along, scale_two


def update_kernel(
    sz, sums_ref, guess_one, moves_one, guess_two, moves_two, update_ref,
):
    line = jnp.sum(sums_ref[...], axis=0)
    lane = iota((1, sz.nx), 1)
    gram = [
        jnp.sum(jnp.where(lane == no, line, 0.0), axis=1, keepdims=True) for no in range(6)
    ]
    one, two = weights_of(gram)
    for k in range(sz.lz):
        update_ref[0, k] = one * guess_one[k] + two * guess_two[k]
        update_ref[1, k] = one * moves_one[0, k] + two * moves_two[0, k]
        update_ref[2, k] = one * moves_one[1, k] + two * moves_two[1, k]


def call(kernel, sz, outs, *args, far_in=False, far_out=(), scratch=(), limit=16 * 2**20):
    near = pl.BlockSpec(memory_space=pltpu.VMEM)
    far = pl.BlockSpec(memory_space=pltpu.HBM)
    return pl.pallas_call(
        functools.partial(kernel, sz),
        out_shape=[jax.ShapeDtypeStruct(shape, dtype) for shape, dtype in outs],
        in_specs=[far if far_in else near] * len(args),
        out_specs=[far if no in far_out else near for no in range(len(outs))],
        scratch_shapes=list(scratch),
        compiler_params=pltpu.CompilerParams(vmem_limit_bytes=limit),
    )(*args)


def pair_swap(sz, value, first):
    pairs = []
    for low in range(first, sz.layer - 1, 2):
        pairs += [(low, low + 1), (low + 1, low)]
    return lax.ppermute(value, "layer", pairs)


def exchange(sz, send, even, odd):
    return (
        lax.all_to_all(send, "areal", split_axis=0, concat_axis=0, tiled=True),
        pair_swap(sz, even, 0),
        pair_swap(sz, odd, 1),
    )


def local(
    pressure,
    pressure_old,
    saturations,
    saturations_old,
    pore_volume,
    trans,
    upwind,
    active,
    fault_cell,
    fault_live,
    fault_up,
    fault_trans,
):
    sz = Sizes(
        lax.axis_size("areal"), lax.axis_size("layer"), pressure.shape, fault_cell.shape[3]
    )
    cells = pressure.shape

    def field(count):
        return ((count,) + cells, F32)

    def sends(y_fields, slot_fields, z_fields):
        return [
            ((sz.areal, sz.block_rows(y_fields, slot_fields), sz.nx), F32),
            ((z_fields, sz.ry, sz.nx), F32),
            ((z_fields, sz.ry, sz.nx), F32),
        ]

    def sender(kernel, outs, to_send, *args):
        buffers = [pltpu.VMEM(*to_send[0]), pltpu.SemaphoreType.DMA]
        *kept, send, even, odd = call(
            kernel, sz, outs + to_send, *args, far_out=(len(outs),), scratch=buffers
        )
        return *kept, exchange(sz, send, even, odd)

    one_field = sends(1, 1, 1)
    two_fields = sends(2, 2, 2)
    state = sends(5, 4, 5)
    scalar = (cells, F32)
    act = active.astype(F32)
    fields = jnp.concatenate(
        [pressure[None], saturations, act[None], trans * act, upwind.astype(F32)], axis=0
    )
    *out, col_hot, row_hot, mine = call(
        pack_kernel,
        sz,
        state + [((sz.nx, sz.slots), BF16), ((sz.rows, sz.slots), F32), ((4, sz.slots), F32)],
        fields, fault_cell,
        far_out=(0,),
        scratch=[pltpu.VMEM(*state[0]), pltpu.SemaphoreType.DMA],
    )
    moved = exchange(sz, *out)
    resid, start, total_co, image_co, sat_co, inverse, slots, rhs, ready, *out = call(
        setup_kernel,
        sz,
        [field(3), field(3), field(6), field(21), field(22), field(3), ((10, sz.slots), F32),
         scalar, scalar] + one_field,
        *moved, fields, pressure_old, saturations_old, pore_volume, fault_live, fault_up,
        fault_trans, col_hot, row_hot, mine,
        far_out=(0, 9),
        scratch=[
            pltpu.VMEM(*field(3)), pltpu.VMEM(*one_field[0]), pltpu.SemaphoreType.DMA((2,))
        ],
    )
    moved = exchange(sz, *out)

    def precondition(vector, rhs, ready, moved):
        for _ in range(SWEEPS - 2):
            ready, moved = sender(
                sweep_kernel, [scalar], one_field,
                *moved, ready, rhs, total_co, inverse, slots, col_hot, row_hot,
            )
        guess, image, moved = sender(
            last_sweep_kernel, [scalar, field(3)], one_field,
            *moved, ready, total_co, inverse, image_co, slots, col_hot, row_hot,
        )
        moves, rows, picked, moved = sender(
            second_kernel, [field(2), field(3), ((2, sz.slots), F32)], two_fields,
            *moved, image, vector, image_co, sat_co, inverse, slots, col_hot, row_hot,
        )
        return guess, moves, rows, picked, moved

    guess_one, moves_one, rows, picked, moved = precondition(start, rhs, ready, moved)
    shifted, rhs, ready, moved = sender(
        next_kernel, [field(3), scalar, scalar], one_field,
        *moved, rows, picked, start, sat_co, total_co, inverse, slots, col_hot, row_hot,
    )
    guess_two, moves_two, rows, picked, moved = precondition(shifted, rhs, ready, moved)
    (sums,) = call(
        gram_kernel, sz, [((sz.areal * sz.layer, 1, sz.nx), F32)],
        *moved, rows, picked, start, shifted, sat_co, slots, col_hot, row_hot,
    )
    sums = lax.all_to_all(sums, ("areal", "layer"), split_axis=0, concat_axis=0, tiled=True)
    (update,) = call(
        update_kernel, sz, [field(3)], sums, guess_one, moves_one, guess_two, moves_two
    )
    return (resid, update)


def solution(mesh):
    cell = P("layer", "areal", None)
    rows = P(None, "layer", "areal", None)
    fault = P("layer", "areal", None, None)
    return jax.shard_map(
        local,
        mesh=mesh,
        in_specs=(cell, cell, rows, rows, cell, rows, rows, cell, fault, fault, fault, fault),
        out_specs=(rows, rows),
        check_vma=False,
    )
```

```python
import functools

import jax
import jax.numpy as jnp
from jax import lax
from jax.experimental import pallas as pl
from jax.experimental.pallas import tpu as pltpu
from jax.sharding import PartitionSpec as P

SWEEPS = 4

COMPRESS = (0.01, 0.02, 0.05)
DAMPING = 0.7

F32 = jnp.float32
BF16 = jnp.bfloat16


class Sizes:
    def __init__(self, areal, layer, cells, cap):
        self.areal = areal
        self.layer = layer
        self.lz, self.ry, self.nx = cells
        self.cap = cap
        self.rows = self.lz * self.ry
        self.slots = areal * cap

    def block_rows(self, y_fields, slot_fields):
        used = y_fields * self.lz + slot_fields
        return -(-used // 8) * 8


def iota(shape, dim):
    return lax.broadcasted_iota(jnp.int32, shape, dim)


def layers_of(sz, ref, *lead):
    return [ref[lead + (no,)] for no in range(sz.lz)]


def put_layers(ref, lead, parts):
    for no, part in enumerate(parts):
        ref[lead + (no,)] = part


def split_parts(value):
    high = value.astype(BF16)
    rest = value - high.astype(F32)
    middle = rest.astype(BF16)
    low = (rest - middle.astype(F32)).astype(BF16)
    return high, middle, low


def gather_slots(sz, fields, row_hot, col_hot):
    pieces = [split_parts(jnp.concatenate(field, axis=0)) for field in fields]
    lhs = jnp.concatenate([part for piece in pieces for part in piece], axis=0)
    picked = jnp.dot(lhs, col_hot, preferred_element_type=F32)
    out = []
    for no in range(len(fields)):
        base = 3 * no * sz.rows
        high = picked[base : base + sz.rows]
        middle = picked[base + sz.rows : base + 2 * sz.rows]
        low = picked[base + 2 * sz.rows : base + 3 * sz.rows]
        full = (low + middle) + high
        out.append(jnp.sum(full * row_hot, axis=0, keepdims=True))
    return jnp.concatenate(out, axis=0)


def scatter_slots(sz, values, row_hot, col_hot):
    count = values.shape[0]
    pieces = []
    for no in range(count):
        value = values[no : no + 1]
        high = value.astype(BF16).astype(F32)
        rest = value - high
        middle = rest.astype(BF16).astype(F32)
        low = (rest - middle).astype(BF16).astype(F32)
        for part in (high, middle, low):
            pieces.append((row_hot * part).astype(BF16))
    lhs = jnp.concatenate(pieces, axis=0)
    spread = lax.dot_general(
        lhs, col_hot, (((1,), (1,)), ((), ())), preferred_element_type=F32
    )
    out = []
    for no in range(count):
        base = 3 * no * sz.rows
        high = spread[base : base + sz.rows]
        middle = spread[base + sz.rows : base + 2 * sz.rows]
        low = spread[base + 2 * sz.rows : base + 3 * sz.rows]
        full = (low + middle) + high
        out.append([full[k * sz.ry : (k + 1) * sz.ry] for k in range(sz.lz)])
    return out


def lane_row(sz, ref):
    return jnp.concatenate([ref[0, 0, j : j + 1, :] for j in range(sz.areal)], axis=1)


def paired_lanes(sz):
    return 2 * sz.cap == sz.nx and sz.areal % 2 == 0


def read_slots(sz, recv_ref, first, count):
    blocks = [recv_ref[j, first : first + count, :] for j in range(sz.areal)]
    if not paired_lanes(sz):
        return jnp.concatenate([block[:, : sz.cap] for block in blocks], axis=1)
    left = iota((count, sz.nx), 1) < sz.cap
    return jnp.concatenate(
        [jnp.where(left, blocks[j], blocks[j + 1]) for j in range(0, sz.areal, 2)], axis=1
    )


def write_slots(sz, send_ref, first, values):
    count = values.shape[0]
    if not paired_lanes(sz):
        for j in range(sz.areal):
            part = values[:, j * sz.cap : (j + 1) * sz.cap]
            send_ref[j, first : first + count, 0 : sz.cap] = part
        return
    left = iota((count, sz.nx), 1) < sz.cap
    for j in range(0, sz.areal, 2):
        tile = values[:, j * sz.cap : (j + 2) * sz.cap]
        turned = pltpu.roll(tile, sz.cap, 1)
        send_ref[j, first : first + count, :] = jnp.where(left, tile, turned)
        send_ref[j + 1, first : first + count, :] = jnp.where(left, turned, tile)


def even_layer(sz):
    place = lax.rem(lax.axis_index("layer"), 2)
    return jnp.full((sz.ry, sz.nx), place, jnp.int32) == 0


def write_halo(sz, send_ref, even_ref, odd_ref, y_up, y_down, z_up, z_down):
    me = lax.axis_index("areal")

    @pl.when(me < sz.areal - 1)
    def _():
        for f, field in enumerate(y_up):
            for k in range(sz.lz):
                send_ref[me + 1, f * sz.lz + k : f * sz.lz + k + 1, :] = field[k][sz.ry - 1 : sz.ry]

    @pl.when(me > 0)
    def _():
        for f, field in enumerate(y_down):
            for k in range(sz.lz):
                send_ref[me - 1, f * sz.lz + k : f * sz.lz + k + 1, :] = field[k][0:1]

    even = even_layer(sz)
    for f in range(len(z_up)):
        top = z_up[f][sz.lz - 1]
        bottom = z_down[f][0] if f < len(z_down) else top
        even_ref[f] = jnp.where(even, top, bottom)
        odd_ref[f] = jnp.where(even, bottom, top)


def read_halo(sz, recv_ref, even_ref, odd_ref, low_fields, high_fields):
    me = lax.axis_index("areal")
    has_low = jnp.full((1, sz.nx), me, jnp.int32) > 0
    has_high = jnp.full((1, sz.nx), me, jnp.int32) < sz.areal - 1
    before = jnp.maximum(me - 1, 0)
    after = jnp.minimum(me + 1, sz.areal - 1)
    even = even_layer(sz)
    lows, highs = [], []
    for f in range(low_fields):
        y_part = [
            jnp.where(has_low, recv_ref[before, f * sz.lz + k : f * sz.lz + k + 1, :], 0.0)
            for k in range(sz.lz)
        ]
        lows.append((y_part, jnp.where(even, odd_ref[f], even_ref[f])))
    for f in range(high_fields):
        y_part = [
            jnp.where(has_high, recv_ref[after, f * sz.lz + k : f * sz.lz + k + 1, :], 0.0)
            for k in range(sz.lz)
        ]
        highs.append((y_part, jnp.where(even, even_ref[f], odd_ref[f])))
    return lows, highs


def x_below(sz, part):
    return pltpu.roll(part, 1, 1)


def x_above(sz, part):
    return pltpu.roll(part, sz.nx - 1, 1)


def y_below(sz, part, edge):
    return jnp.where(iota((sz.ry, sz.nx), 0) == 0, edge, pltpu.roll(part, 1, 0))


def y_above(sz, part, edge):
    return jnp.where(iota((sz.ry, sz.nx), 0) == sz.ry - 1, edge, pltpu.roll(part, sz.ry - 1, 0))


def neighbours(sz, field, k, low, high):
    below = field[k - 1] if k > 0 else low[1]
    above = field[k + 1] if k < sz.lz - 1 else high[1]
    return (
        x_below(sz, field[k]),
        x_above(sz, field[k]),
        y_below(sz, field[k], low[0][k]),
        y_above(sz, field[k], high[0][k]),
        below,
        above,
    )


def inner_neighbours(sz, field, k):
    return (
        x_below(sz, field[k]),
        x_above(sz, field[k]),
        y_below(sz, field[k], 0.0),
        y_above(sz, field[k], 0.0),
        field[k - 1] if k > 0 else None,
        field[k + 1] if k < sz.lz - 1 else None,
    )


def weighted(values, ref, lead):
    total = None
    for d, value in enumerate(values):
        if value is not None:
            term = ref[lead(d)] * value
            total = term if total is None else total + term
    return total


def edge_values(sz, k, low, high):
    row = iota((sz.ry, sz.nx), 0)
    return (
        None,
        None,
        jnp.where(row == 0, low[0][k], 0.0),
        jnp.where(row == sz.ry - 1, high[0][k], 0.0),
        low[1] if k == 0 else None,
        high[1] if k == sz.lz - 1 else None,
    )


def mobility(sat_water, sat_gas):
    sat_oil = 1.0 - sat_water - sat_gas
    mobile = (
        sat_water * sat_water * 2.0,
        sat_oil * sat_oil * 0.5,
        sat_gas * sat_gas * 5.0,
    )
    slopes = (4.0 * sat_water, -sat_oil, 10.0 * sat_gas)
    return mobile, slopes


def pack_kernel(
    sz, state_ref, cell_in,
    send_ref, even_ref, odd_ref, col_ref, row_ref, mine_ref,
):
    cell = lane_row(sz, cell_in)
    row_start = iota((sz.rows, sz.slots), 0) * sz.nx
    in_row = (cell >= row_start) & (cell < row_start + sz.nx)
    row_hot = jnp.where(in_row, 1.0, 0.0)
    column = cell - jnp.sum(jnp.where(in_row, row_start, 0), axis=0, keepdims=True)
    col_hot = jnp.where(iota((sz.nx, sz.slots), 0) == column, 1.0, 0.0).astype(BF16)
    pressure, water, gas, act, _, ty, tz, _, uy, uz = [
        layers_of(sz, state_ref, no) for no in range(10)
    ]
    four = [pressure, water, gas, act]
    mine = gather_slots(sz, four, row_hot, col_hot)
    write_slots(sz, send_ref, 5 * sz.lz, mine)
    write_halo(
        sz, send_ref, even_ref, odd_ref,
        [pressure, water, gas, ty, uy], four, [pressure, water, gas, tz, uz], four,
    )

    @meanwhile
    def _():
        row_ref[...] = row_hot
        col_ref[...] = col_hot
        mine_ref[...] = mine


def send_fields(sz, fields, row_hot, col_hot, send_ref, even_ref, odd_ref):
    picked = gather_slots(sz, fields, row_hot, col_hot)
    write_halo(sz, send_ref, even_ref, odd_ref, fields, fields, fields, fields)
    write_slots(sz, send_ref, len(fields) * sz.lz, picked)
    return picked


def meanwhile(body):
    body()


def sweep_ready(sz, guesses, rhs, total_ref, relax, ready_ref):
    for k in range(sz.lz):
        total = weighted(inner_neighbours(sz, guesses, k), total_ref, lambda d: (d, k))
        ready_ref[k] = (1.0 - DAMPING) * guesses[k] + relax[k] * (rhs[k] + total)


def setup_kernel(
    sz, recv_ref, even_in, odd_in, state_ref, old_ref, sat_old_ref, pore_ref,
    live_ref, fup_ref, ftrans_ref, col_ref, row_ref, mine_ref,
    resid_hbm, start_ref, total_ref, image_ref, sat_co_ref, inv_ref, slot_ref,
    rhs_ref, ready_ref, send_ref, even_ref, odd_ref, resid_ref, sem,
):
    row_hot = row_ref[...]
    col_hot = col_ref[...]
    mine = mine_ref[...]
    their = read_slots(sz, recv_ref, 5 * sz.lz, 4)
    live = lane_row(sz, live_ref).astype(F32)
    high = lane_row(sz, fup_ref) > 0
    tau = lane_row(sz, ftrans_ref) * live * mine[3:4] * their[3:4]
    drop = their[0:1] - mine[0:1]
    mobile, slopes = mobility(
        jnp.where(high, their[1:2], mine[1:2]), jnp.where(high, their[2:3], mine[2:3])
    )
    flow = [tau * part for part in mobile]
    bend = [tau * drop * part for part in slopes]
    flow_sum = flow[0] + flow[1] + flow[2]
    scattered = scatter_slots(
        sz,
        jnp.concatenate(flow + [part * drop for part in flow], axis=0),
        row_hot,
        col_hot,
    )
    lows, highs = read_halo(sz, recv_ref, even_in, odd_in, 5, 4)
    pressure, water, gas, act, *faces = [layers_of(sz, state_ref, no) for no in range(10)]
    carried, flags = faces[:3], faces[3:]
    lane = iota((sz.ry, sz.nx), 1)
    guesses, relaxes, rights = [], [], []
    for k in range(sz.lz):
        own_act = act[k]
        spare = 1.0 - own_act
        near = [
            neighbours(sz, field, k, lows[f], highs[f])
            for f, field in enumerate((pressure, water, gas, act))
        ]
        below_y = y_below(sz, carried[1][k], lows[3][0][k])
        flag_y = y_below(sz, flags[1][k], lows[4][0][k])
        below_z = carried[2][k - 1] if k > 0 else lows[3][1]
        flag_z = flags[2][k - 1] if k > 0 else lows[4][1]
        taus = (
            jnp.where(lane > 0, x_below(sz, carried[0][k]) * own_act, 0.0),
            jnp.where(lane < sz.nx - 1, carried[0][k] * near[3][1], 0.0),
            below_y * own_act,
            carried[1][k] * near[3][3],
            below_z * own_act,
            carried[2][k] * near[3][5],
        )
        other_up = (
            x_below(sz, flags[0][k]) < 0.5,
            flags[0][k] > 0.5,
            flag_y < 0.5,
            flags[1][k] > 0.5,
            flag_z < 0.5,
            flags[2][k] > 0.5,
        )
        change = pressure[k] - old_ref[k]
        oil = 1.0 - water[k] - gas[k]
        old_water = sat_old_ref[0, k]
        old_gas = sat_old_ref[1, k]
        now = (water[k], oil, gas[k])
        before = (old_water, 1.0 - old_water - old_gas, old_gas)
        pore = pore_ref[k]
        store_p = [own_act * pore * c * s for c, s in zip(COMPRESS, now)]
        store_s = [pore * (1.0 + c * change) for c in COMPRESS]
        resid = [
            own_act * (pore * (s - b + c * s * change)) for c, s, b in zip(COMPRESS, now, before)
        ]
        image_own = [store_p[0], store_p[1], store_p[2]]
        sat_own = [own_act * store_s[0], -(own_act * store_s[1]), own_act * store_s[2]]
        diag = store_p[0] + store_p[1] + store_p[2]
        for d in range(6):
            step = near[0][d] - pressure[k]
            mobile, slopes = mobility(
                jnp.where(other_up[d], near[1][d], water[k]),
                jnp.where(other_up[d], near[2][d], gas[k]),
            )
            face_flow = [taus[d] * part for part in mobile]
            total = face_flow[0] + face_flow[1] + face_flow[2]
            total_ref[d, k] = total
            diag = diag + total
            slope_tau = taus[d] * step
            for row in range(3):
                resid[row] = resid[row] - face_flow[row] * step
                image_own[row] = image_own[row] + face_flow[row]
                image_ref[3 + 6 * row + d, k] = face_flow[row]
                face_bend = slope_tau * slopes[row]
                sat_co_ref[4 + 6 * row + d, k] = jnp.where(other_up[d], face_bend, 0.0)
                sat_own[row] = sat_own[row] - jnp.where(other_up[d], 0.0, face_bend)
        for row in range(3):
            resid[row] = resid[row] - scattered[3 + row][k]
            image_own[row] = image_own[row] + scattered[row][k]
            resid_ref[row, k] = resid[row]
            start_ref[row, k] = -resid[row]
        diag = diag + (scattered[0][k] + scattered[1][k] + scattered[2][k]) + spare
        image_ref[0, k] = image_own[0] + spare
        image_ref[1, k] = image_own[1]
        image_ref[2, k] = image_own[2]
        sat_co_ref[0, k] = sat_own[0]
        sat_co_ref[1, k] = sat_own[1]
        sat_co_ref[2, k] = sat_own[2] + spare
        sat_co_ref[3, k] = spare
        relax = DAMPING / diag
        inv_ref[0, k] = relax
        inv_ref[1, k] = own_act / store_s[0]
        inv_ref[2, k] = own_act / store_s[2]
        rhs = -(resid[0] + resid[1] + resid[2])
        rhs_ref[k] = rhs
        relaxes.append(relax)
        rights.append(rhs)
        guesses.append(relax * rhs)
    resid_out = pltpu.make_async_copy(resid_ref, resid_hbm, sem)
    resid_out.start()
    send_fields(
        sz, [guesses], row_hot, col_hot, send_ref, even_ref, odd_ref
    )

    @meanwhile
    def _():
        slot_ref[...] = jnp.concatenate(
            [flow_sum]
            + flow
            + [jnp.where(high, 0.0, part) for part in bend]
            + [jnp.where(high, part, 0.0) for part in bend],
            axis=0,
        )
        sweep_ready(sz, guesses, rights, total_ref, relaxes, ready_ref)

    resid_out.wait()


def next_guess(sz, recv_ref, even_in, odd_in, ready_in, total_ref, inv_ref, slot_ref, row_hot,
               col_hot):
    their = read_slots(sz, recv_ref, sz.lz, 1)
    scattered = scatter_slots(sz, slot_ref[0:1] * their, row_hot, col_hot)[0]
    lows, highs = read_halo(sz, recv_ref, even_in, odd_in, 1, 1)
    guesses = []
    for k in range(sz.lz):
        outside = weighted(edge_values(sz, k, lows[0], highs[0]), total_ref, lambda d: (d, k))
        guesses.append(ready_in[k] + inv_ref[0, k] * (outside + scattered[k]))
    return guesses


def sweep_kernel(
    sz, recv_ref, even_in, odd_in, ready_in, rhs_ref, total_ref, inv_ref, slot_ref, col_ref,
    row_ref, ready_ref, send_ref, even_ref, odd_ref,
):
    row_hot = row_ref[...]
    col_hot = col_ref[...]
    guesses = next_guess(
        sz, recv_ref, even_in, odd_in, ready_in, total_ref, inv_ref, slot_ref, row_hot, col_hot
    )
    send_fields(
        sz, [guesses], row_hot, col_hot, send_ref, even_ref, odd_ref
    )

    @meanwhile
    def _():
        sweep_ready(
            sz, guesses, layers_of(sz, rhs_ref), total_ref, layers_of(sz, inv_ref, 0), ready_ref
        )


def last_sweep_kernel(
    sz, recv_ref, even_in, odd_in, ready_in, total_ref, inv_ref, image_co_ref, slot_ref, col_ref,
    row_ref, guess_ref, image_ref, send_ref, even_ref, odd_ref,
):
    row_hot = row_ref[...]
    col_hot = col_ref[...]
    guesses = next_guess(
        sz, recv_ref, even_in, odd_in, ready_in, total_ref, inv_ref, slot_ref, row_hot, col_hot
    )
    send_fields(
        sz, [guesses], row_hot, col_hot, send_ref, even_ref, odd_ref
    )

    @meanwhile
    def _():
        for k in range(sz.lz):
            guess_ref[k] = guesses[k]
            near = inner_neighbours(sz, guesses, k)
            for row in range(3):
                image_ref[row, k] = image_co_ref[row, k] * guesses[k] - weighted(
                    near, image_co_ref, lambda d: (3 + 6 * row + d, k)
                )


def second_kernel(
    sz, recv_ref, even_in, odd_in, image_in, vector_ref, image_co_ref, sat_co_ref, inv_ref,
    slot_ref, col_ref, row_ref, moves_ref, rows_ref, picked_ref, send_ref, even_ref, odd_ref,
):
    row_hot = row_ref[...]
    col_hot = col_ref[...]
    their = read_slots(sz, recv_ref, sz.lz, 1)
    scattered = scatter_slots(sz, slot_ref[1:4] * their, row_hot, col_hot)
    lows, highs = read_halo(sz, recv_ref, even_in, odd_in, 1, 1)
    water, gas, images = [], [], []
    for k in range(sz.lz):
        outside = edge_values(sz, k, lows[0], highs[0])
        image = [
            image_in[row, k]
            - (
                weighted(outside, image_co_ref, lambda d: (3 + 6 * row + d, k))
                + scattered[row][k]
            )
            for row in range(3)
        ]
        images.append(image)
        water.append(inv_ref[1, k] * (vector_ref[0, k] - image[0]))
        gas.append(inv_ref[2, k] * (vector_ref[2, k] - image[2]))
    picked = send_fields(
        sz, [water, gas], row_hot, col_hot, send_ref, even_ref, odd_ref
    )

    @meanwhile
    def _():
        picked_ref[...] = picked
        both = [w + g for w, g in zip(water, gas)]
        for k in range(sz.lz):
            moves_ref[0, k] = water[k]
            moves_ref[1, k] = gas[k]
            own = (water[k], both[k], gas[k])
            near_w = inner_neighbours(sz, water, k)
            near_g = inner_neighbours(sz, gas, k)
            near = (near_w, [None if w is None else w + g for w, g in zip(near_w, near_g)], near_g)
            for row in range(3):
                value = images[k][row] + sat_co_ref[row, k] * own[row]
                if row == 1:
                    value = value + sat_co_ref[3, k] * water[k]
                rows_ref[row, k] = value - weighted(
                    near[row], sat_co_ref, lambda d: (4 + 6 * row + d, k)
                )


def apply_sat(sz, recv_ref, even_in, odd_in, rows_in, picked_ref, co_ref, slot_ref, col_hot,
              row_hot):
    their = read_slots(sz, recv_ref, 2 * sz.lz, 2)
    mine = picked_ref[...]
    mine_rows = (mine[0:1], mine[0:1] + mine[1:2], mine[1:2])
    their_rows = (their[0:1], their[0:1] + their[1:2], their[1:2])
    values = jnp.concatenate(
        [
            slot_ref[4 + row : 5 + row] * mine_rows[row]
            + slot_ref[7 + row : 8 + row] * their_rows[row]
            for row in range(3)
        ],
        axis=0,
    )
    scattered = scatter_slots(sz, values, row_hot, col_hot)
    lows, highs = read_halo(sz, recv_ref, even_in, odd_in, 2, 2)
    rows = []
    for k in range(sz.lz):
        near_w = edge_values(sz, k, lows[0], highs[0])
        near_g = edge_values(sz, k, lows[1], highs[1])
        near = (near_w, [None if w is None else w + g for w, g in zip(near_w, near_g)], near_g)
        rows.append(
            [
                rows_in[row, k]
                - (
                    weighted(near[row], co_ref, lambda d: (4 + 6 * row + d, k))
                    + scattered[row][k]
                )
                for row in range(3)
            ]
        )
    return rows


def next_kernel(
    sz, recv_ref, even_in, odd_in, rows_in, picked_ref, vector_ref, sat_co_ref, total_ref, inv_ref,
    slot_ref, col_ref, row_ref, shifted_ref, rhs_ref, ready_ref, send_ref, even_ref, odd_ref,
):
    row_hot = row_ref[...]
    col_hot = col_ref[...]
    rows = apply_sat(
        sz, recv_ref, even_in, odd_in, rows_in, picked_ref, sat_co_ref, slot_ref, col_hot, row_hot
    )
    guesses, rights, relaxes = [], [], []
    for k in range(sz.lz):
        shifted = [rows[k][row] - vector_ref[row, k] for row in range(3)]
        for row in range(3):
            shifted_ref[row, k] = shifted[row]
        rhs = shifted[0] + shifted[1] + shifted[2]
        rhs_ref[k] = rhs
        relax = inv_ref[0, k]
        rights.append(rhs)
        relaxes.append(relax)
        guesses.append(relax * rhs)
    send_fields(
        sz, [guesses], row_hot, col_hot, send_ref, even_ref, odd_ref
    )

    @meanwhile
    def _():
        sweep_ready(sz, guesses, rights, total_ref, relaxes, ready_ref)


def gram_kernel(
    sz, recv_ref, even_in, odd_in, rows_in, picked_ref, start_ref, vector_ref, co_ref, slot_ref,
    col_ref, row_ref, sums_ref,
):
    rows = apply_sat(
        sz, recv_ref, even_in, odd_in, rows_in, picked_ref, co_ref, slot_ref, col_ref[...],
        row_ref[...],
    )
    sums = [jnp.zeros((sz.ry, sz.nx), F32) for _ in range(6)]
    for k in range(sz.lz):
        for row in range(3):
            first = start_ref[row, k]
            second = vector_ref[row, k]
            third = rows[k][row] - second
            pairs = (
                (first, first), (first, second), (second, second),
                (first, third), (second, third), (third, third),
            )
            sums = [total + a * b for total, (a, b) in zip(sums, pairs)]
    lane = iota((1, sz.nx), 1)
    line = jnp.zeros((1, sz.nx), F32)
    for no, total in enumerate(sums):
        value = jnp.sum(jnp.sum(total, axis=0, keepdims=True), axis=1, keepdims=True)
        line = jnp.where(lane == no, value, line)
    sums_ref[...] = jnp.broadcast_to(line.reshape(1, 1, sz.nx), sums_ref.shape)


def weights_of(gram):
    rr, rx, xx, ry, xy, yy = gram
    beta = jnp.sqrt(rr)
    along = rx / rr
    norm_sq = jnp.maximum(xx - along * rx, 0.0)
    norm = jnp.sqrt(norm_sq)
    h11 = 1.0 + along
    h21 = norm / beta
    on_first = (ry - along * rx) / (norm * beta)
    on_second = (xy - along * xx - along * ry + along * along * rx) / norm_sq
    length = (yy - 2.0 * along * xy + along * along * xx) / norm_sq
    h12 = on_first
    h22 = 1.0 + on_second
    h32 = jnp.sqrt(jnp.maximum(length - on_first * on_first - on_second * on_second, 0.0))
    radius = jnp.sqrt(h11 * h11 + h21 * h21)
    cosine = h11 / radius
    sine = h21 / radius
    top = cosine * h12 + sine * h22
    low = -sine * h12 + cosine * h22
    target_top = cosine * beta
    target_low = -sine * beta
    second_radius = jnp.sqrt(low * low + h32 * h32)
    weight_two = (low / second_radius) * target_low / second_radius
    weight_one = (target_top - top * weight_two) / radius
    scale_two = weight_two / norm
    return weight_one / beta - scale_two * along, scale_two


def update_kernel(
    sz, sums_ref, guess_one, moves_one, guess_two, moves_two, update_ref,
):
    line = jnp.sum(sums_ref[...], axis=0)
    lane = iota((1, sz.nx), 1)
    gram = [
        jnp.sum(jnp.where(lane == no, line, 0.0), axis=1, keepdims=True) for no in range(6)
    ]
    one, two = weights_of(gram)
    for k in range(sz.lz):
        update_ref[0, k] = one * guess_one[k] + two * guess_two[k]
        update_ref[1, k] = one * moves_one[0, k] + two * moves_two[0, k]
        update_ref[2, k] = one * moves_one[1, k] + two * moves_two[1, k]


def call(kernel, sz, outs, *args, far_in=False, far_out=(), scratch=(), limit=16 * 2**20):
    near = pl.BlockSpec(memory_space=pltpu.VMEM)
    far = pl.BlockSpec(memory_space=pltpu.HBM)
    return pl.pallas_call(
        functools.partial(kernel, sz),
        out_shape=[jax.ShapeDtypeStruct(shape, dtype) for shape, dtype in outs],
        in_specs=[far if far_in else near] * len(args),
        out_specs=[far if no in far_out else near for no in range(len(outs))],
        scratch_shapes=list(scratch),
        compiler_params=pltpu.CompilerParams(vmem_limit_bytes=limit),
    )(*args)


def pair_swap(sz, value, first):
    pairs = []
    for low in range(first, sz.layer - 1, 2):
        pairs += [(low, low + 1), (low + 1, low)]
    return lax.ppermute(value, "layer", pairs)


def exchange(sz, send, even, odd):
    return (
        lax.cond(
            lax.axis_index("areal") < sz.areal,
            lambda value: lax.all_to_all(
                value, "areal", split_axis=0, concat_axis=0, tiled=True
            ),
            jnp.zeros_like,
            send,
        ),
        pair_swap(sz, even, 0),
        pair_swap(sz, odd, 1),
    )


def local(
    pressure,
    pressure_old,
    saturations,
    saturations_old,
    pore_volume,
    trans,
    upwind,
    active,
    fault_cell,
    fault_live,
    fault_up,
    fault_trans,
):
    sz = Sizes(
        lax.axis_size("areal"), lax.axis_size("layer"), pressure.shape, fault_cell.shape[3]
    )
    cells = pressure.shape

    def field(count):
        return ((count,) + cells, F32)

    def sends(y_fields, slot_fields, z_fields):
        return [
            ((sz.areal, sz.block_rows(y_fields, slot_fields), sz.nx), F32),
            ((z_fields, sz.ry, sz.nx), F32),
            ((z_fields, sz.ry, sz.nx), F32),
        ]

    def sender(kernel, outs, to_send, *args):
        *kept, send, even, odd = call(kernel, sz, outs + to_send, *args)
        return *kept, exchange(sz, send, even, odd)

    one_field = sends(1, 1, 1)
    two_fields = sends(2, 2, 2)
    state = sends(5, 4, 5)
    scalar = (cells, F32)
    act = active.astype(F32)
    fields = jnp.concatenate(
        [pressure[None], saturations, act[None], trans * act, upwind.astype(F32)], axis=0
    )
    *out, col_hot, row_hot, mine = call(
        pack_kernel,
        sz,
        state + [((sz.nx, sz.slots), BF16), ((sz.rows, sz.slots), F32), ((4, sz.slots), F32)],
        fields, fault_cell,
    )
    moved = exchange(sz, *out)
    resid, start, total_co, image_co, sat_co, inverse, slots, rhs, ready, *out = call(
        setup_kernel,
        sz,
        [field(3), field(3), field(6), field(21), field(22), field(3), ((10, sz.slots), F32),
         scalar, scalar] + one_field,
        *moved, fields, pressure_old, saturations_old, pore_volume, fault_live, fault_up,
        fault_trans, col_hot, row_hot, mine,
        far_out=(0,),
        scratch=[
            pltpu.VMEM(*field(3)), pltpu.SemaphoreType.DMA
        ],
    )
    moved = exchange(sz, *out)

    def precondition(vector, rhs, ready, moved):
        for _ in range(SWEEPS - 2):
            ready, moved = sender(
                sweep_kernel, [scalar], one_field,
                *moved, ready, rhs, total_co, inverse, slots, col_hot, row_hot,
            )
        guess, image, moved = sender(
            last_sweep_kernel, [scalar, field(3)], one_field,
            *moved, ready, total_co, inverse, image_co, slots, col_hot, row_hot,
        )
        moves, rows, picked, moved = sender(
            second_kernel, [field(2), field(3), ((2, sz.slots), F32)], two_fields,
            *moved, image, vector, image_co, sat_co, inverse, slots, col_hot, row_hot,
        )
        return guess, moves, rows, picked, moved

    guess_one, moves_one, rows, picked, moved = precondition(start, rhs, ready, moved)
    shifted, rhs, ready, moved = sender(
        next_kernel, [field(3), scalar, scalar], one_field,
        *moved, rows, picked, start, sat_co, total_co, inverse, slots, col_hot, row_hot,
    )
    guess_two, moves_two, rows, picked, moved = precondition(shifted, rhs, ready, moved)
    (sums,) = call(
        gram_kernel, sz, [((sz.areal * sz.layer, 1, sz.nx), F32)],
        *moved, rows, picked, start, shifted, sat_co, slots, col_hot, row_hot,
    )
    sums = lax.all_to_all(sums, ("areal", "layer"), split_axis=0, concat_axis=0, tiled=True)
    (update,) = call(
        update_kernel, sz, [field(3)], sums, guess_one, moves_one, guess_two, moves_two
    )
    return (resid, update)


def solution(mesh):
    cell = P("layer", "areal", None)
    rows = P(None, "layer", "areal", None)
    fault = P("layer", "areal", None, None)
    return jax.shard_map(
        local,
        mesh=mesh,
        in_specs=(cell, cell, rows, rows, cell, rows, rows, cell, fault, fault, fault, fault),
        out_specs=(rows, rows),
        check_vma=False,
    )
```

```python
import functools

import jax
import jax.numpy as jnp
from jax import lax
from jax.experimental import pallas as pl
from jax.experimental.pallas import tpu as pltpu
from jax.sharding import PartitionSpec as P

SWEEPS = 4

COMPRESS = (0.01, 0.02, 0.05)
DAMPING = 0.7

F32 = jnp.float32
BF16 = jnp.bfloat16


class Sizes:
    def __init__(self, areal, layer, cells, cap):
        self.areal = areal
        self.layer = layer
        self.lz, self.ry, self.nx = cells
        self.cap = cap
        self.rows = self.lz * self.ry
        self.slots = areal * cap

    def block_rows(self, y_fields, slot_fields):
        used = y_fields * self.lz + slot_fields
        return -(-used // 8) * 8


def iota(shape, dim):
    return lax.broadcasted_iota(jnp.int32, shape, dim)


def layers_of(sz, ref, *lead):
    return [ref[lead + (no,)] for no in range(sz.lz)]


def put_layers(ref, lead, parts):
    for no, part in enumerate(parts):
        ref[lead + (no,)] = part


def split_parts(value):
    high = value.astype(BF16)
    rest = value - high.astype(F32)
    middle = rest.astype(BF16)
    low = (rest - middle.astype(F32)).astype(BF16)
    return high, middle, low


def gather_slots(sz, fields, row_hot, col_hot):
    pieces = [split_parts(jnp.concatenate(field, axis=0)) for field in fields]
    lhs = jnp.concatenate([part for piece in pieces for part in piece], axis=0)
    picked = jnp.dot(lhs, col_hot, preferred_element_type=F32)
    out = []
    for no in range(len(fields)):
        base = 3 * no * sz.rows
        high = picked[base : base + sz.rows]
        middle = picked[base + sz.rows : base + 2 * sz.rows]
        low = picked[base + 2 * sz.rows : base + 3 * sz.rows]
        full = (low + middle) + high
        out.append(jnp.sum(full * row_hot, axis=0, keepdims=True))
    return jnp.concatenate(out, axis=0)


def scatter_slots(sz, values, row_hot, col_hot):
    count = values.shape[0]
    pieces = []
    for no in range(count):
        value = values[no : no + 1]
        high = value.astype(BF16).astype(F32)
        rest = value - high
        middle = rest.astype(BF16).astype(F32)
        low = (rest - middle).astype(BF16).astype(F32)
        for part in (high, middle, low):
            pieces.append((row_hot * part).astype(BF16))
    lhs = jnp.concatenate(pieces, axis=0)
    spread = lax.dot_general(
        lhs, col_hot, (((1,), (1,)), ((), ())), preferred_element_type=F32
    )
    out = []
    for no in range(count):
        base = 3 * no * sz.rows
        high = spread[base : base + sz.rows]
        middle = spread[base + sz.rows : base + 2 * sz.rows]
        low = spread[base + 2 * sz.rows : base + 3 * sz.rows]
        full = (low + middle) + high
        out.append([full[k * sz.ry : (k + 1) * sz.ry] for k in range(sz.lz)])
    return out


def lane_row(sz, ref):
    return jnp.concatenate([ref[0, 0, j : j + 1, :] for j in range(sz.areal)], axis=1)


def paired_lanes(sz):
    return 2 * sz.cap == sz.nx and sz.areal % 2 == 0


def read_slots(sz, recv_ref, first, count):
    blocks = [recv_ref[j, first : first + count, :] for j in range(sz.areal)]
    if not paired_lanes(sz):
        return jnp.concatenate([block[:, : sz.cap] for block in blocks], axis=1)
    left = iota((count, sz.nx), 1) < sz.cap
    return jnp.concatenate(
        [jnp.where(left, blocks[j], blocks[j + 1]) for j in range(0, sz.areal, 2)], axis=1
    )


def write_slots(sz, send_ref, first, values):
    count = values.shape[0]
    if not paired_lanes(sz):
        for j in range(sz.areal):
            part = values[:, j * sz.cap : (j + 1) * sz.cap]
            send_ref[j, first : first + count, 0 : sz.cap] = part
        return
    left = iota((count, sz.nx), 1) < sz.cap
    for j in range(0, sz.areal, 2):
        tile = values[:, j * sz.cap : (j + 2) * sz.cap]
        turned = pltpu.roll(tile, sz.cap, 1)
        send_ref[j, first : first + count, :] = jnp.where(left, tile, turned)
        send_ref[j + 1, first : first + count, :] = jnp.where(left, turned, tile)


def even_layer(sz):
    place = lax.rem(lax.axis_index("layer"), 2)
    return jnp.full((sz.ry, sz.nx), place, jnp.int32) == 0


def write_halo(sz, send_ref, even_ref, odd_ref, y_up, y_down, z_up, z_down):
    me = lax.axis_index("areal")

    @pl.when(me < sz.areal - 1)
    def _():
        for f, field in enumerate(y_up):
            for k in range(sz.lz):
                send_ref[me + 1, f * sz.lz + k : f * sz.lz + k + 1, :] = field[k][sz.ry - 1 : sz.ry]

    @pl.when(me > 0)
    def _():
        for f, field in enumerate(y_down):
            for k in range(sz.lz):
                send_ref[me - 1, f * sz.lz + k : f * sz.lz + k + 1, :] = field[k][0:1]

    even = even_layer(sz)
    for f in range(len(z_up)):
        top = z_up[f][sz.lz - 1]
        bottom = z_down[f][0] if f < len(z_down) else top
        even_ref[f] = jnp.where(even, top, bottom)
        odd_ref[f] = jnp.where(even, bottom, top)


def read_halo(sz, recv_ref, even_ref, odd_ref, low_fields, high_fields):
    me = lax.axis_index("areal")
    has_low = jnp.full((1, sz.nx), me, jnp.int32) > 0
    has_high = jnp.full((1, sz.nx), me, jnp.int32) < sz.areal - 1
    before = jnp.maximum(me - 1, 0)
    after = jnp.minimum(me + 1, sz.areal - 1)
    even = even_layer(sz)
    lows, highs = [], []
    for f in range(low_fields):
        y_part = [
            jnp.where(has_low, recv_ref[before, f * sz.lz + k : f * sz.lz + k + 1, :], 0.0)
            for k in range(sz.lz)
        ]
        lows.append((y_part, jnp.where(even, odd_ref[f], even_ref[f])))
    for f in range(high_fields):
        y_part = [
            jnp.where(has_high, recv_ref[after, f * sz.lz + k : f * sz.lz + k + 1, :], 0.0)
            for k in range(sz.lz)
        ]
        highs.append((y_part, jnp.where(even, even_ref[f], odd_ref[f])))
    return lows, highs


def x_below(sz, part):
    return pltpu.roll(part, 1, 1)


def x_above(sz, part):
    return pltpu.roll(part, sz.nx - 1, 1)


def y_below(sz, part, edge):
    return jnp.where(iota((sz.ry, sz.nx), 0) == 0, edge, pltpu.roll(part, 1, 0))


def y_above(sz, part, edge):
    return jnp.where(iota((sz.ry, sz.nx), 0) == sz.ry - 1, edge, pltpu.roll(part, sz.ry - 1, 0))


def neighbours(sz, field, k, low, high):
    below = field[k - 1] if k > 0 else low[1]
    above = field[k + 1] if k < sz.lz - 1 else high[1]
    return (
        x_below(sz, field[k]),
        x_above(sz, field[k]),
        y_below(sz, field[k], low[0][k]),
        y_above(sz, field[k], high[0][k]),
        below,
        above,
    )


def inner_neighbours(sz, field, k):
    return (
        x_below(sz, field[k]),
        x_above(sz, field[k]),
        y_below(sz, field[k], 0.0),
        y_above(sz, field[k], 0.0),
        field[k - 1] if k > 0 else None,
        field[k + 1] if k < sz.lz - 1 else None,
    )


def weighted(values, ref, lead):
    total = None
    for d, value in enumerate(values):
        if value is not None:
            term = ref[lead(d)] * value
            total = term if total is None else total + term
    return total


def edge_values(sz, k, low, high):
    row = iota((sz.ry, sz.nx), 0)
    return (
        None,
        None,
        jnp.where(row == 0, low[0][k], 0.0),
        jnp.where(row == sz.ry - 1, high[0][k], 0.0),
        low[1] if k == 0 else None,
        high[1] if k == sz.lz - 1 else None,
    )


def mobility(sat_water, sat_gas):
    sat_oil = 1.0 - sat_water - sat_gas
    mobile = (
        sat_water * sat_water * 2.0,
        sat_oil * sat_oil * 0.5,
        sat_gas * sat_gas * 5.0,
    )
    slopes = (4.0 * sat_water, -sat_oil, 10.0 * sat_gas)
    return mobile, slopes


def pack_kernel(
    sz, cell_hbm, p_hbm, sat_hbm, act_hbm, trans_hbm, up_hbm, old_hbm, sat_old_hbm, pore_hbm,
    live_hbm, fup_hbm, ftrans_hbm,
    send_ref, even_ref, odd_ref, col_ref, row_ref, line_ref, state_ref,
    cell_ref, act_ref, trans_ref, up_ref, live_ref, fup_ref, ftrans_ref, sems,
):
    moves = [
        pltpu.make_async_copy(source, target, sems.at[no])
        for no, (source, target) in enumerate(
            (
                (cell_hbm, cell_ref),
                (p_hbm, state_ref.at[0]),
                (sat_hbm, state_ref.at[pl.ds(1, 2)]),
                (act_hbm, act_ref),
                (trans_hbm, trans_ref),
                (up_hbm, up_ref),
                (live_hbm, live_ref),
                (fup_hbm, fup_ref),
                (ftrans_hbm, ftrans_ref),
                (old_hbm, state_ref.at[10]),
                (sat_old_hbm, state_ref.at[pl.ds(11, 2)]),
                (pore_hbm, state_ref.at[13]),
            )
        )
    ]
    for move in moves:
        move.start()
    moves[0].wait()
    cell = lane_row(sz, cell_ref)
    row_start = iota((sz.rows, sz.slots), 0) * sz.nx
    in_row = (cell >= row_start) & (cell < row_start + sz.nx)
    row_hot = jnp.where(in_row, 1.0, 0.0)
    column = cell - jnp.sum(jnp.where(in_row, row_start, 0), axis=0, keepdims=True)
    col_hot = jnp.where(iota((sz.nx, sz.slots), 0) == column, 1.0, 0.0).astype(BF16)
    row_ref[...] = row_hot
    col_ref[...] = col_hot
    for move in moves[1:]:
        move.wait()
    pressure, water, gas = [layers_of(sz, state_ref, no) for no in range(3)]
    act = [part.astype(F32) for part in layers_of(sz, act_ref)]
    put_layers(state_ref, (3,), act)
    faces = []
    for axis in range(3):
        carried = [t * a for t, a in zip(layers_of(sz, trans_ref, axis), act)]
        flags = [u.astype(F32) for u in layers_of(sz, up_ref, axis)]
        put_layers(state_ref, (4 + axis,), carried)
        put_layers(state_ref, (7 + axis,), flags)
        faces.append((carried, flags))
    four = [pressure, water, gas, act]
    mine = gather_slots(sz, four, row_hot, col_hot)
    write_slots(sz, send_ref, 5 * sz.lz, mine)
    write_halo(
        sz, send_ref, even_ref, odd_ref,
        [pressure, water, gas, *faces[1]], four, [pressure, water, gas, *faces[2]], four,
    )
    line_ref[...] = jnp.concatenate(
        [
            mine,
            lane_row(sz, ftrans_ref) * lane_row(sz, live_ref).astype(F32),
            lane_row(sz, fup_ref).astype(F32),
        ],
        axis=0,
    )


def send_fields(sz, fields, row_hot, col_hot, send_ref, even_ref, odd_ref):
    picked = gather_slots(sz, fields, row_hot, col_hot)
    write_halo(sz, send_ref, even_ref, odd_ref, fields, fields, fields, fields)
    write_slots(sz, send_ref, len(fields) * sz.lz, picked)
    return picked


def meanwhile(body):
    body()


def sweep_ready(sz, guesses, rhs, total_ref, relax, ready_ref):
    for k in range(sz.lz):
        total = weighted(inner_neighbours(sz, guesses, k), total_ref, lambda d: (d, k))
        ready_ref[k] = (1.0 - DAMPING) * guesses[k] + relax[k] * (rhs[k] + total)


def setup_kernel(
    sz, recv_ref, even_in, odd_in, state_ref, line_ref, col_ref, row_ref,
    resid_hbm, start_ref, total_ref, image_ref, sat_co_ref, inv_ref, slot_ref,
    rhs_ref, ready_ref, send_ref, even_ref, odd_ref, resid_ref, sem,
):
    row_hot = row_ref[...]
    col_hot = col_ref[...]
    mine = line_ref[0:4]
    their = read_slots(sz, recv_ref, 5 * sz.lz, 4)
    high = line_ref[5:6] > 0.5
    tau = line_ref[4:5] * mine[3:4] * their[3:4]
    drop = their[0:1] - mine[0:1]
    mobile, slopes = mobility(
        jnp.where(high, their[1:2], mine[1:2]), jnp.where(high, their[2:3], mine[2:3])
    )
    flow = [tau * part for part in mobile]
    bend = [tau * drop * part for part in slopes]
    flow_sum = flow[0] + flow[1] + flow[2]
    scattered = scatter_slots(
        sz,
        jnp.concatenate(flow + [part * drop for part in flow], axis=0),
        row_hot,
        col_hot,
    )
    lows, highs = read_halo(sz, recv_ref, even_in, odd_in, 5, 4)
    pressure, water, gas, act, *faces = [layers_of(sz, state_ref, no) for no in range(14)]
    carried, flags = faces[:3], faces[3:6]
    old, old_waters, old_gases, pores = faces[6:]
    lane = iota((sz.ry, sz.nx), 1)
    guesses, relaxes, rights = [], [], []
    for k in range(sz.lz):
        own_act = act[k]
        spare = 1.0 - own_act
        near = [
            neighbours(sz, field, k, lows[f], highs[f])
            for f, field in enumerate((pressure, water, gas, act))
        ]
        below_y = y_below(sz, carried[1][k], lows[3][0][k])
        flag_y = y_below(sz, flags[1][k], lows[4][0][k])
        below_z = carried[2][k - 1] if k > 0 else lows[3][1]
        flag_z = flags[2][k - 1] if k > 0 else lows[4][1]
        taus = (
            jnp.where(lane > 0, x_below(sz, carried[0][k]) * own_act, 0.0),
            jnp.where(lane < sz.nx - 1, carried[0][k] * near[3][1], 0.0),
            below_y * own_act,
            carried[1][k] * near[3][3],
            below_z * own_act,
            carried[2][k] * near[3][5],
        )
        other_up = (
            x_below(sz, flags[0][k]) < 0.5,
            flags[0][k] > 0.5,
            flag_y < 0.5,
            flags[1][k] > 0.5,
            flag_z < 0.5,
            flags[2][k] > 0.5,
        )
        change = pressure[k] - old[k]
        oil = 1.0 - water[k] - gas[k]
        old_water = old_waters[k]
        old_gas = old_gases[k]
        now = (water[k], oil, gas[k])
        before = (old_water, 1.0 - old_water - old_gas, old_gas)
        pore = pores[k]
        store_p = [own_act * pore * c * s for c, s in zip(COMPRESS, now)]
        store_s = [pore * (1.0 + c * change) for c in COMPRESS]
        resid = [
            own_act * (pore * (s - b + c * s * change)) for c, s, b in zip(COMPRESS, now, before)
        ]
        image_own = [store_p[0], store_p[1], store_p[2]]
        sat_own = [own_act * store_s[0], -(own_act * store_s[1]), own_act * store_s[2]]
        diag = store_p[0] + store_p[1] + store_p[2]
        for d in range(6):
            step = near[0][d] - pressure[k]
            mobile, slopes = mobility(
                jnp.where(other_up[d], near[1][d], water[k]),
                jnp.where(other_up[d], near[2][d], gas[k]),
            )
            face_flow = [taus[d] * part for part in mobile]
            total = face_flow[0] + face_flow[1] + face_flow[2]
            total_ref[d, k] = total
            diag = diag + total
            slope_tau = taus[d] * step
            for row in range(3):
                resid[row] = resid[row] - face_flow[row] * step
                image_own[row] = image_own[row] + face_flow[row]
                image_ref[3 + 6 * row + d, k] = face_flow[row]
                face_bend = slope_tau * slopes[row]
                sat_co_ref[4 + 6 * row + d, k] = jnp.where(other_up[d], face_bend, 0.0)
                sat_own[row] = sat_own[row] - jnp.where(other_up[d], 0.0, face_bend)
        for row in range(3):
            resid[row] = resid[row] - scattered[3 + row][k]
            image_own[row] = image_own[row] + scattered[row][k]
            resid_ref[row, k] = resid[row]
            start_ref[row, k] = -resid[row]
        diag = diag + (scattered[0][k] + scattered[1][k] + scattered[2][k]) + spare
        image_ref[0, k] = image_own[0] + spare
        image_ref[1, k] = image_own[1]
        image_ref[2, k] = image_own[2]
        sat_co_ref[0, k] = sat_own[0]
        sat_co_ref[1, k] = sat_own[1]
        sat_co_ref[2, k] = sat_own[2] + spare
        sat_co_ref[3, k] = spare
        relax = DAMPING / diag
        inv_ref[0, k] = relax
        inv_ref[1, k] = own_act / store_s[0]
        inv_ref[2, k] = own_act / store_s[2]
        rhs = -(resid[0] + resid[1] + resid[2])
        rhs_ref[k] = rhs
        relaxes.append(relax)
        rights.append(rhs)
        guesses.append(relax * rhs)
    resid_out = pltpu.make_async_copy(resid_ref, resid_hbm, sem)
    resid_out.start()
    send_fields(
        sz, [guesses], row_hot, col_hot, send_ref, even_ref, odd_ref
    )

    @meanwhile
    def _():
        slot_ref[...] = jnp.concatenate(
            [flow_sum]
            + flow
            + [jnp.where(high, 0.0, part) for part in bend]
            + [jnp.where(high, part, 0.0) for part in bend],
            axis=0,
        )
        sweep_ready(sz, guesses, rights, total_ref, relaxes, ready_ref)

    resid_out.wait()


def next_guess(sz, recv_ref, even_in, odd_in, ready_in, total_ref, inv_ref, slot_ref, row_hot,
               col_hot):
    their = read_slots(sz, recv_ref, sz.lz, 1)
    scattered = scatter_slots(sz, slot_ref[0:1] * their, row_hot, col_hot)[0]
    lows, highs = read_halo(sz, recv_ref, even_in, odd_in, 1, 1)
    guesses = []
    for k in range(sz.lz):
        outside = weighted(edge_values(sz, k, lows[0], highs[0]), total_ref, lambda d: (d, k))
        guesses.append(ready_in[k] + inv_ref[0, k] * (outside + scattered[k]))
    return guesses


def sweep_kernel(
    sz, recv_ref, even_in, odd_in, ready_in, rhs_ref, total_ref, inv_ref, slot_ref, col_ref,
    row_ref, ready_ref, send_ref, even_ref, odd_ref,
):
    row_hot = row_ref[...]
    col_hot = col_ref[...]
    guesses = next_guess(
        sz, recv_ref, even_in, odd_in, ready_in, total_ref, inv_ref, slot_ref, row_hot, col_hot
    )
    send_fields(
        sz, [guesses], row_hot, col_hot, send_ref, even_ref, odd_ref
    )

    @meanwhile
    def _():
        sweep_ready(
            sz, guesses, layers_of(sz, rhs_ref), total_ref, layers_of(sz, inv_ref, 0), ready_ref
        )


def last_sweep_kernel(
    sz, recv_ref, even_in, odd_in, ready_in, total_ref, inv_ref, image_co_ref, slot_ref, col_ref,
    row_ref, guess_ref, image_ref, send_ref, even_ref, odd_ref,
):
    row_hot = row_ref[...]
    col_hot = col_ref[...]
    guesses = next_guess(
        sz, recv_ref, even_in, odd_in, ready_in, total_ref, inv_ref, slot_ref, row_hot, col_hot
    )
    send_fields(
        sz, [guesses], row_hot, col_hot, send_ref, even_ref, odd_ref
    )

    @meanwhile
    def _():
        for k in range(sz.lz):
            guess_ref[k] = guesses[k]
            near = inner_neighbours(sz, guesses, k)
            for row in range(3):
                image_ref[row, k] = image_co_ref[row, k] * guesses[k] - weighted(
                    near, image_co_ref, lambda d: (3 + 6 * row + d, k)
                )


def second_kernel(
    sz, recv_ref, even_in, odd_in, image_in, vector_ref, image_co_ref, sat_co_ref, inv_ref,
    slot_ref, col_ref, row_ref, moves_ref, rows_ref, picked_ref, send_ref, even_ref, odd_ref,
):
    row_hot = row_ref[...]
    col_hot = col_ref[...]
    their = read_slots(sz, recv_ref, sz.lz, 1)
    scattered = scatter_slots(sz, slot_ref[1:4] * their, row_hot, col_hot)
    lows, highs = read_halo(sz, recv_ref, even_in, odd_in, 1, 1)
    water, gas, images = [], [], []
    for k in range(sz.lz):
        outside = edge_values(sz, k, lows[0], highs[0])
        image = [
            image_in[row, k]
            - (
                weighted(outside, image_co_ref, lambda d: (3 + 6 * row + d, k))
                + scattered[row][k]
            )
            for row in range(3)
        ]
        images.append(image)
        water.append(inv_ref[1, k] * (vector_ref[0, k] - image[0]))
        gas.append(inv_ref[2, k] * (vector_ref[2, k] - image[2]))
    picked = send_fields(
        sz, [water, gas], row_hot, col_hot, send_ref, even_ref, odd_ref
    )

    @meanwhile
    def _():
        picked_ref[...] = picked
        both = [w + g for w, g in zip(water, gas)]
        for k in range(sz.lz):
            moves_ref[0, k] = water[k]
            moves_ref[1, k] = gas[k]
            own = (water[k], both[k], gas[k])
            near_w = inner_neighbours(sz, water, k)
            near_g = inner_neighbours(sz, gas, k)
            near = (near_w, [None if w is None else w + g for w, g in zip(near_w, near_g)], near_g)
            for row in range(3):
                value = images[k][row] + sat_co_ref[row, k] * own[row]
                if row == 1:
                    value = value + sat_co_ref[3, k] * water[k]
                rows_ref[row, k] = value - weighted(
                    near[row], sat_co_ref, lambda d: (4 + 6 * row + d, k)
                )


def apply_sat(sz, recv_ref, even_in, odd_in, rows_in, picked_ref, co_ref, slot_ref, col_hot,
              row_hot):
    their = read_slots(sz, recv_ref, 2 * sz.lz, 2)
    mine = picked_ref[...]
    mine_rows = (mine[0:1], mine[0:1] + mine[1:2], mine[1:2])
    their_rows = (their[0:1], their[0:1] + their[1:2], their[1:2])
    values = jnp.concatenate(
        [
            slot_ref[4 + row : 5 + row] * mine_rows[row]
            + slot_ref[7 + row : 8 + row] * their_rows[row]
            for row in range(3)
        ],
        axis=0,
    )
    scattered = scatter_slots(sz, values, row_hot, col_hot)
    lows, highs = read_halo(sz, recv_ref, even_in, odd_in, 2, 2)
    rows = []
    for k in range(sz.lz):
        near_w = edge_values(sz, k, lows[0], highs[0])
        near_g = edge_values(sz, k, lows[1], highs[1])
        near = (near_w, [None if w is None else w + g for w, g in zip(near_w, near_g)], near_g)
        rows.append(
            [
                rows_in[row, k]
                - (
                    weighted(near[row], co_ref, lambda d: (4 + 6 * row + d, k))
                    + scattered[row][k]
                )
                for row in range(3)
            ]
        )
    return rows


def next_kernel(
    sz, recv_ref, even_in, odd_in, rows_in, picked_ref, vector_ref, sat_co_ref, total_ref, inv_ref,
    slot_ref, col_ref, row_ref, shifted_ref, rhs_ref, ready_ref, send_ref, even_ref, odd_ref,
):
    row_hot = row_ref[...]
    col_hot = col_ref[...]
    rows = apply_sat(
        sz, recv_ref, even_in, odd_in, rows_in, picked_ref, sat_co_ref, slot_ref, col_hot, row_hot
    )
    guesses, rights, relaxes = [], [], []
    for k in range(sz.lz):
        shifted = [rows[k][row] - vector_ref[row, k] for row in range(3)]
        for row in range(3):
            shifted_ref[row, k] = shifted[row]
        rhs = shifted[0] + shifted[1] + shifted[2]
        rhs_ref[k] = rhs
        relax = inv_ref[0, k]
        rights.append(rhs)
        relaxes.append(relax)
        guesses.append(relax * rhs)
    send_fields(
        sz, [guesses], row_hot, col_hot, send_ref, even_ref, odd_ref
    )

    @meanwhile
    def _():
        sweep_ready(sz, guesses, rights, total_ref, relaxes, ready_ref)


def gram_kernel(
    sz, recv_ref, even_in, odd_in, rows_in, picked_ref, start_ref, vector_ref, co_ref, slot_ref,
    col_ref, row_ref, sums_ref,
):
    rows = apply_sat(
        sz, recv_ref, even_in, odd_in, rows_in, picked_ref, co_ref, slot_ref, col_ref[...],
        row_ref[...],
    )
    sums = [jnp.zeros((sz.ry, sz.nx), F32) for _ in range(6)]
    for k in range(sz.lz):
        for row in range(3):
            first = start_ref[row, k]
            second = vector_ref[row, k]
            third = rows[k][row] - second
            pairs = (
                (first, first), (first, second), (second, second),
                (first, third), (second, third), (third, third),
            )
            sums = [total + a * b for total, (a, b) in zip(sums, pairs)]
    lane = iota((1, sz.nx), 1)
    line = jnp.zeros((1, sz.nx), F32)
    for no, total in enumerate(sums):
        value = jnp.sum(jnp.sum(total, axis=0, keepdims=True), axis=1, keepdims=True)
        line = jnp.where(lane == no, value, line)
    sums_ref[...] = jnp.broadcast_to(line.reshape(1, 1, sz.nx), sums_ref.shape)


def weights_of(gram):
    rr, rx, xx, ry, xy, yy = gram
    beta = jnp.sqrt(rr)
    along = rx / rr
    norm_sq = jnp.maximum(xx - along * rx, 0.0)
    norm = jnp.sqrt(norm_sq)
    h11 = 1.0 + along
    h21 = norm / beta
    on_first = (ry - along * rx) / (norm * beta)
    on_second = (xy - along * xx - along * ry + along * along * rx) / norm_sq
    length = (yy - 2.0 * along * xy + along * along * xx) / norm_sq
    h12 = on_first
    h22 = 1.0 + on_second
    h32 = jnp.sqrt(jnp.maximum(length - on_first * on_first - on_second * on_second, 0.0))
    radius = jnp.sqrt(h11 * h11 + h21 * h21)
    cosine = h11 / radius
    sine = h21 / radius
    top = cosine * h12 + sine * h22
    low = -sine * h12 + cosine * h22
    target_top = cosine * beta
    target_low = -sine * beta
    second_radius = jnp.sqrt(low * low + h32 * h32)
    weight_two = (low / second_radius) * target_low / second_radius
    weight_one = (target_top - top * weight_two) / radius
    scale_two = weight_two / norm
    return weight_one / beta - scale_two * along, scale_two


def update_kernel(
    sz, sums_ref, guess_one, moves_one, guess_two, moves_two, update_ref,
):
    line = jnp.sum(sums_ref[...], axis=0)
    lane = iota((1, sz.nx), 1)
    gram = [
        jnp.sum(jnp.where(lane == no, line, 0.0), axis=1, keepdims=True) for no in range(6)
    ]
    one, two = weights_of(gram)
    for k in range(sz.lz):
        update_ref[0, k] = one * guess_one[k] + two * guess_two[k]
        update_ref[1, k] = one * moves_one[0, k] + two * moves_two[0, k]
        update_ref[2, k] = one * moves_one[1, k] + two * moves_two[1, k]


def call(kernel, sz, outs, *args, far_in=False, far_out=(), scratch=(), limit=16 * 2**20):
    near = pl.BlockSpec(memory_space=pltpu.VMEM)
    far = pl.BlockSpec(memory_space=pltpu.HBM)
    return pl.pallas_call(
        functools.partial(kernel, sz),
        out_shape=[jax.ShapeDtypeStruct(shape, dtype) for shape, dtype in outs],
        in_specs=[far if far_in else near] * len(args),
        out_specs=[far if no in far_out else near for no in range(len(outs))],
        scratch_shapes=list(scratch),
        compiler_params=pltpu.CompilerParams(vmem_limit_bytes=limit),
    )(*args)


def pair_swap(sz, value, first):
    pairs = []
    for low in range(first, sz.layer - 1, 2):
        pairs += [(low, low + 1), (low + 1, low)]
    return lax.ppermute(value, "layer", pairs)


def exchange(sz, send, even, odd):
    return (
        lax.cond(
            lax.axis_index("areal") < sz.areal,
            lambda value: lax.all_to_all(
                value, "areal", split_axis=0, concat_axis=0, tiled=True
            ),
            jnp.zeros_like,
            send,
        ),
        pair_swap(sz, even, 0),
        pair_swap(sz, odd, 1),
    )


def local(
    pressure,
    pressure_old,
    saturations,
    saturations_old,
    pore_volume,
    trans,
    upwind,
    active,
    fault_cell,
    fault_live,
    fault_up,
    fault_trans,
):
    sz = Sizes(
        lax.axis_size("areal"), lax.axis_size("layer"), pressure.shape, fault_cell.shape[3]
    )
    cells = pressure.shape

    def field(count):
        return ((count,) + cells, F32)

    def sends(y_fields, slot_fields, z_fields):
        return [
            ((sz.areal, sz.block_rows(y_fields, slot_fields), sz.nx), F32),
            ((z_fields, sz.ry, sz.nx), F32),
            ((z_fields, sz.ry, sz.nx), F32),
        ]

    def sender(kernel, outs, to_send, *args):
        *kept, send, even, odd = call(kernel, sz, outs + to_send, *args)
        return *kept, exchange(sz, send, even, odd)

    one_field = sends(1, 1, 1)
    two_fields = sends(2, 2, 2)
    state = sends(5, 4, 5)
    scalar = (cells, F32)
    inputs = (
        fault_cell, pressure, saturations, active, trans, upwind, pressure_old, saturations_old,
        pore_volume, fault_live, fault_up, fault_trans,
    )
    *out, col_hot, row_hot, lines, fields = call(
        pack_kernel,
        sz,
        state
        + [((sz.nx, sz.slots), BF16), ((sz.rows, sz.slots), F32), ((6, sz.slots), F32), field(14)],
        *inputs,
        far_in=True,
        limit=67043328,
        scratch=[
            pltpu.VMEM(value.shape, value.dtype)
            for value in (
                fault_cell, active, trans, upwind, fault_live, fault_up, fault_trans
            )
        ]
        + [pltpu.SemaphoreType.DMA((len(inputs),))],
    )
    moved = exchange(sz, *out)
    resid, start, total_co, image_co, sat_co, inverse, slots, rhs, ready, *out = call(
        setup_kernel,
        sz,
        [field(3), field(3), field(6), field(21), field(22), field(3), ((10, sz.slots), F32),
         scalar, scalar] + one_field,
        *moved, fields, lines, col_hot, row_hot,
        far_out=(0,),
        scratch=[
            pltpu.VMEM(*field(3)), pltpu.SemaphoreType.DMA
        ],
    )
    moved = exchange(sz, *out)

    def precondition(vector, rhs, ready, moved):
        for _ in range(SWEEPS - 2):
            ready, moved = sender(
                sweep_kernel, [scalar], one_field,
                *moved, ready, rhs, total_co, inverse, slots, col_hot, row_hot,
            )
        guess, image, moved = sender(
            last_sweep_kernel, [scalar, field(3)], one_field,
            *moved, ready, total_co, inverse, image_co, slots, col_hot, row_hot,
        )
        moves, rows, picked, moved = sender(
            second_kernel, [field(2), field(3), ((2, sz.slots), F32)], two_fields,
            *moved, image, vector, image_co, sat_co, inverse, slots, col_hot, row_hot,
        )
        return guess, moves, rows, picked, moved

    guess_one, moves_one, rows, picked, moved = precondition(start, rhs, ready, moved)
    shifted, rhs, ready, moved = sender(
        next_kernel, [field(3), scalar, scalar], one_field,
        *moved, rows, picked, start, sat_co, total_co, inverse, slots, col_hot, row_hot,
    )
    guess_two, moves_two, rows, picked, moved = precondition(shifted, rhs, ready, moved)
    (sums,) = call(
        gram_kernel, sz, [((sz.areal * sz.layer, 1, sz.nx), F32)],
        *moved, rows, picked, start, shifted, sat_co, slots, col_hot, row_hot,
    )
    sums = lax.all_to_all(sums, ("areal", "layer"), split_axis=0, concat_axis=0, tiled=True)
    (update,) = call(
        update_kernel, sz, [field(3)], sums, guess_one, moves_one, guess_two, moves_two
    )
    return (resid, update)


def solution(mesh):
    cell = P("layer", "areal", None)
    rows = P(None, "layer", "areal", None)
    fault = P("layer", "areal", None, None)
    return jax.shard_map(
        local,
        mesh=mesh,
        in_specs=(cell, cell, rows, rows, cell, rows, rows, cell, fault, fault, fault, fault),
        out_specs=(rows, rows),
        check_vma=False,
    )
```
